512 devices in a mesh: scen: 32 (over y, x, core), space: 8 (over z_lo), tm: 2 (over z_hi).
Axes of the slice: x: 4, y: 4, z: 16 (z_hi: 2, z_lo: 8; z = z_hi * 8 + z_lo), core: 2. Of those that a mesh axis runs over, the one named last changes fastest.
Arguments:
- coupling: bfloat16 [32, 4, 8, 128, 512], P('scen', 'tm', 'space'), may hold values from -0.09375 to 0.09375
- leaf_rhs: float32 [32, 4, 8, 128], P('scen', 'tm', 'space'), may hold values from -6 to 6
- conductance: float32 [32, 4, 8, 128], P('scen', 'tm', 'space'), may hold values from 0.42 to 0.52
- compressor: int32 [32, 4, 8], P('scen', 'tm', 'space'), may hold values 0 or 1
- blocks: float32 [32, 4, 8, 128, 128], P('scen', 'tm', 'space'), may hold values from -2 to 8, as said below
- parent_of: int32 [32], P('scen'), may hold values from 0 to 7, as said below
- parent_mat: float32 [8, 512, 512], P(None, ('space', 'tm')), may hold values from -2 to 8, as said below
- parent_rhs: float32 [8, 512], P(None, ('space', 'tm')), may hold values from -6 to 6
- link: float32 [8, 512, 256], P(None, ('space', 'tm')), may hold values from -0.25 to 0.25
- root_mat: float32 [256, 256], replicated, may hold values from -2 to 8, as said below
- root_rhs: float32 [256], replicated, may hold values from -6 to 6
Outputs:
- leaf_move: float32 [32, 4, 8, 128], P('scen', 'tm', 'space')
- parent_at_leaf: float32 [32, 512], P('scen', ('space', 'tm'))
- root_step: float32 [256], replicated
The draws below stay inside these ranges and needn't reach their ends.
Inputs may be any that keep to these rules, and one draw needn't show every extreme that they name: `parent_of`: leaves come in aligned runs of 4 in a row; all leaves of a run share one parent, and each parent owns exactly one run. `blocks`: each block is symmetric with eigenvalues of 1 or more. `parent_mat`: each matrix is symmetric with eigenvalues of 1 or more. `root_mat`: symmetric with eigenvalues of 1 or more.
All inputs are finite; a program needn't handle non-finite values. No bound on the sum of `compressor` on one device may be relied on, other than what follows from the above.
Results may differ from the reference program's by a relative error of at most 0.0003.
Values sent between devices are 32-bit elements; how exact they have to be, the bound alone decides.
No kernel may reach another device: no remote copies, remote signals or barrier semaphores. Data moves between devices by JAX's collectives and lax.ppermute only.
A program may use at most 64 MiB of HBM per device.

```python
import jax
import jax.numpy as jnp
from jax import lax

PB = 128
NC = 512
NR = 256
PARENTS = 8
ITERS = 6
LEAVES = 32
NT = 4
NS = 8


def symmetric_gram(key, shape, order):
    base = jax.random.normal(key, shape, jnp.float32)
    return jnp.einsum('...ij,...kj->...ik', base, base) / order


def draw_blocks(key, part):
    gram = symmetric_gram(key, (LEAVES, NT, NS, PB, PB), 4.0 * PB)
    return gram + jnp.eye(PB, dtype=jnp.float32)


def draw_parent_of(key, part):
    order = jax.random.permutation(key, PARENTS)
    return order[jnp.arange(LEAVES) // (LEAVES // PARENTS)].astype(jnp.int32)


def draw_parent_mat(key, part):
    gram = symmetric_gram(key, (PARENTS, NC, NC), 1.0 * NC)
    return gram + jnp.eye(NC, dtype=jnp.float32)


def draw_root_mat(key, part):
    gram = symmetric_gram(key, (NR, NR), 1.0 * NR)
    return gram + jnp.eye(NR, dtype=jnp.float32)


def with_ends(result, key, least, largest):
    index_at = [jax.random.randint(jax.random.fold_in(key, axis), (), 0, length) for axis, length in enumerate(result.shape)]
    widest = result.shape.index(max(result.shape))
    next_to = index_at[:widest] + [(index_at[widest] + 1) % result.shape[widest]] + index_at[widest + 1:]
    return result.at[tuple(index_at)].set(least).at[tuple(next_to)].set(largest)


def level_of(rng, extent, split, low, high):
    gain, own = 1.0, jax.random.fold_in(rng, 6)
    for axis_at, blocks in split:
        draws = jnp.exp(jax.random.uniform(jax.random.fold_in(own, axis_at), (blocks,), jnp.float32, low / len(split), high / len(split)))
        gain = gain * jnp.repeat(draws, extent[axis_at] // blocks).reshape([-1 if axis == axis_at else 1 for axis in range(len(extent))])
    return gain


def bell_draw(rng, shape, spread, limit, shards=(), kind=jnp.bfloat16):
    drawn = jax.random.normal(rng, shape, jnp.float32) * spread
    if len(shards) > 0:
        drawn = level_of(rng, shape, shards, -0.22, 0.18) * drawn
    return jnp.clip(drawn, min=-limit, max=limit).astype(kind)


def setup_inputs(seed: int = 0) -> dict:
    key_of = jax.random.split(jax.random.key(seed), 12)
    coupling = bell_draw(key_of[0], (LEAVES, NT, NS, PB, NC), (NT * NS * PB) ** -0.5, 0.09375, ((0, 32), (1, 2), (2, 8)))
    leaf_rhs = bell_draw(key_of[1], (LEAVES, NT, NS, PB), 1.0, 6.0, ((0, 32), (1, 2), (2, 8)), jnp.float32)
    conductance = jnp.clip(0.42 + 0.099999994 * jax.random.uniform(key_of[2], (LEAVES, NT, NS, PB), jnp.float32) ** level_of(key_of[2], (LEAVES, NT, NS, PB), ((0, 32), (1, 2), (2, 8)), -0.2, 0.2), 0.42, 0.52)
    compressor = with_ends((jax.random.randint(key_of[3], (LEAVES, NT, NS), 0, 4) < 3).astype(jnp.int32), jax.random.fold_in(key_of[3], 1), 0, 1)
    blocks = draw_blocks(jax.random.fold_in(key_of[11], 71), 0)
    parent_of = draw_parent_of(jax.random.fold_in(key_of[11], 71), 0)
    parent_mat = draw_parent_mat(jax.random.fold_in(key_of[11], 71), 0)
    parent_rhs = bell_draw(key_of[7], (PARENTS, NC), 1.0, 6.0, ((1, 16),), jnp.float32)
    link = bell_draw(key_of[8], (PARENTS, NC, NR), NC ** -0.5, 0.25, ((1, 16),), jnp.float32)
    root_mat = draw_root_mat(jax.random.fold_in(key_of[11], 71), 0)
    root_rhs = bell_draw(key_of[10], (NR,), 1.0, 6.0, (), jnp.float32)
    return dict(coupling=coupling, leaf_rhs=leaf_rhs, conductance=conductance, compressor=compressor, blocks=blocks, parent_of=parent_of, parent_mat=parent_mat, parent_rhs=parent_rhs, link=link, root_mat=root_mat, root_rhs=root_rhs)


HIGH = lax.Precision.HIGHEST

def factor_solve(matrix, right):
    factor = lax.linalg.cholesky(matrix)
    forward = lax.linalg.triangular_solve(factor, right, left_side=True, lower=True)
    return lax.linalg.triangular_solve(factor, forward, left_side=True, lower=True, transpose_a=True)

def invert_blocks(matrices):
    identity = jnp.broadcast_to(jnp.eye(matrices.shape[-1], dtype=matrices.dtype), matrices.shape)
    return factor_solve(matrices, identity)

def beside_all(padded):
    return padded[2:, 1:-1] + padded[:-2, 1:-1] + padded[1:-1, 2:] + padded[1:-1, :-2]

def couple(field, weight):
    scale = weight
    if field.ndim == 4:
        scale = weight[..., None]
    widths = [(1, 1), (1, 1)] + [(0, 0)] * (field.ndim - 2)
    return beside_all(jnp.pad(field * scale, widths)) * scale

def block_apply(inverse, field):
    if field.ndim == 4:
        return jnp.einsum('tsij,tsjc->tsic', inverse, field, precision=HIGH)
    return jnp.einsum('tsij,tsj->tsi', inverse, field, precision=HIGH)

def jacobi(source, inverse, weight):
    field = block_apply(inverse, source)
    for sweep_index in range(ITERS - 1):
        field = block_apply(inverse, source + couple(field, weight))
    return field

def reference(coupling, leaf_rhs, conductance, compressor, blocks, parent_of, parent_mat, parent_rhs, link, root_mat, root_rhs):
    weight = conductance * (1.0 + compressor.astype(jnp.float32)[..., None]) * 0.5
    inverse = invert_blocks(blocks)

    def leaf_terms(leaf_items):
        dense, right, leaf_weight, leaf_inverse = leaf_items
        dense = dense.astype(jnp.float32)
        solved = jacobi(dense, leaf_inverse, leaf_weight)
        pulled = jacobi(right, leaf_inverse, leaf_weight)
        schur = jnp.einsum('tsic,tsid->cd', dense, solved, precision=HIGH)
        gather_term = jnp.einsum('tsic,tsi->c', dense, pulled, precision=HIGH)
        return (schur, gather_term)
    schur, pulled = lax.map(leaf_terms, (coupling, leaf_rhs, weight, inverse))
    onehot = (parent_of[:, None] == jnp.arange(PARENTS, dtype=jnp.int32)[None, :]).astype(jnp.float32)
    hessian = parent_mat + jnp.einsum('lp,lij->pij', onehot, schur, precision=HIGH)
    reduced = jnp.einsum('lp,li->pi', onehot, pulled, precision=HIGH) - parent_rhs
    link_solved = factor_solve(hessian, link)
    vector_solved = factor_solve(hessian, reduced[..., None])[..., 0]
    root_matrix = root_mat + jnp.einsum('pin,pim->nm', link, link_solved, precision=HIGH)
    root_right = root_rhs - jnp.einsum('pin,pi->n', link, vector_solved, precision=HIGH)
    root_step = factor_solve(root_matrix, root_right[:, None])[:, 0]
    parent_step = vector_solved + jnp.einsum('pin,n->pi', link_solved, root_step, precision=HIGH)
    parent_at_leaf = jnp.einsum('lp,pi->li', onehot, parent_step, precision=HIGH)

    def leaf_step(leaf_items):
        dense, right, leaf_weight, leaf_inverse, target = leaf_items
        source = right - jnp.einsum('tsic,c->tsi', dense.astype(jnp.float32), target, precision=HIGH)
        return jacobi(source, leaf_inverse, leaf_weight)
    leaf_move = lax.map(leaf_step, (coupling, leaf_rhs, weight, inverse, parent_at_leaf))
    return (leaf_move, parent_at_leaf, root_step)
```

```python
import functools

import jax
import jax.numpy as jnp
from jax import lax
from jax.experimental import pallas as pl
from jax.experimental.pallas import tpu as pltpu
from jax.sharding import PartitionSpec as P

AXES = ("scen", "space", "tm")
Z_AXES = ("space", "tm")
F32 = jnp.float32
HIGH = lax.Precision.HIGHEST

QUARTER = (0, 2, 1, 3)
LEAF_OF_QUARTER = (0, 2, 1, 3)
Z_SHIFT = 2


def linear(scen, z):
    return (scen * 8 + z % 8) * 2 + z // 8


def home(group, leaf, half, cell):
    return linear(group * 4 + leaf, half * 8 + cell)


def away(group, leaf, half, cell):
    column = half ^ (leaf // 2)
    z = (4 * QUARTER[leaf] + 3 - cell // 2 + Z_SHIFT) % 16
    return linear(group * 4 + column * 2 + cell % 2, z)


def every_cell():
    for group in range(8):
        for leaf in range(4):
            for half in range(2):
                for cell in range(8):
                    yield group, leaf, half, cell


MOVE_OUT = [(home(*at), away(*at)) for at in every_cell()]
MOVE_BACK = [(there, here) for here, there in MOVE_OUT]
TO_CORE = [(away(g, l, h, c), away(g, l, h, c ^ 1)) for g, l, h, c in every_cell()]
TO_HALF = [(away(g, l, h, c), away(g, l, h ^ 1, c)) for g, l, h, c in every_cell()]
TO_CHIP = [
    (away(g, l, h, c), away(g, l, h, c + (1 if c % 2 else -1)))
    for g, l, h, c in every_cell()
    if 0 <= c + (1 if c % 2 else -1) < 8
]


def flip(bit):
    return [(i, i ^ bit) for i in range(32)]


def dot(a, b, dims=((1,), (0,)), precision=HIGH):
    return lax.dot_general(a, b, (dims, ((), ())), precision=precision, preferred_element_type=F32)


NT = ((1,), (1,))
TN = ((0,), (0,))


def sweep8(matrix, lane, sub):
    top = matrix[:8]
    columns = [jnp.broadcast_to(matrix[:, k : k + 1], (128, 128)) for k in range(8)]
    small = [c[:8] for c in columns]
    rows = jnp.where(lane < 8, (sub == lane).astype(F32), top)
    for k in range(8):
        scale = 1.0 / small[k][k : k + 1]
        pivot_row = rows[k : k + 1] * scale
        factor = jnp.where(sub == k, 0.0, small[k])
        rows = jnp.where(sub == k, pivot_row, rows - factor * pivot_row)
        for j in range(k + 1, 8):
            entry = small[j][k : k + 1] * scale
            small[j] = jnp.where(sub == k, entry, small[j] - factor * entry)
    rest = jnp.where(lane < 8, 0.0, matrix[8:])
    for k in range(8):
        rest = rest - columns[k][8:] * rows[k : k + 1]
    return jnp.concatenate([rest, rows], axis=0)


def inverses(matrices):
    lane = lax.broadcasted_iota(jnp.int32, (1, 128), 1)
    sub = lax.broadcasted_iota(jnp.int32, (8, 1), 0)

    def step(_, carry):
        return tuple(pltpu.roll(sweep8(m, lane, sub), 120, 1) for m in carry)

    return lax.fori_loop(0, 16, step, tuple(matrices))


def call(kernel, name, shapes, *operands, scratch=(), scalars=0):
    smem = pl.BlockSpec(memory_space=pltpu.SMEM)
    vmem = pl.BlockSpec(memory_space=pltpu.VMEM)
    return pl.pallas_call(
        kernel,
        name=name,
        out_shape=[jax.ShapeDtypeStruct(s, F32) for s in shapes],
        in_specs=[smem] * scalars + [vmem] * (len(operands) - scalars),
        out_specs=[vmem] * len(shapes),
        scratch_shapes=list(scratch),
    )(*operands)


def invert_kernel(pack, inverse, scaled, half_scaled):
    found = inverses([pack[0:128], pack[128:256]])
    for t in range(2):
        across = jnp.broadcast_to(pack[258 + t : 259 + t], (128, 128))
        down = across.T
        rows = slice(t * 128, t * 128 + 128)
        inverse[rows] = found[t]
        half_scaled[rows] = down * found[t]
        scaled[rows] = down * found[t] * across


def put_rows(out, first, second):
    out[256:264] = jnp.zeros((8, 512), F32)
    out[256:257, 0:128] = first
    out[256:257, 128:256] = second


def put_half(half, out, blocks, rows):
    early = half == 0
    out[0:128] = jnp.where(early, blocks[1], blocks[0])
    out[128:136] = jnp.zeros((8, 512), F32)
    out[128:129, 0:128] = jnp.where(early, rows[1], rows[0])


def start_kernel(flags, pack, inverse, half_scaled, coupling, first, message, to_half):
    blocks, rows = [], []
    for t in range(2):
        at = slice(t * 128, t * 128 + 128)
        first[at] = dot(inverse[at], coupling[at])
        blocks.append(dot(half_scaled[at], coupling[at]))
        message[at] = blocks[t]
        rows.append(dot(pack[256 + t : 257 + t], half_scaled[at], NT))
    put_rows(message, *rows)
    put_half(flags[0], to_half, blocks, rows)


def beside(half, own, core, chip, other):
    late = (half == 1).astype(F32)
    weights = (late, 1.0 - late)
    blocks, rows = [], []
    for t in range(2):
        at = slice(t * 128, t * 128 + 128)
        back = slice(128 - t * 128, 256 - t * 128)
        blocks.append(own[back] + core[at] + chip[at] + other[0:128] * weights[t])
        rows.append(
            own[256:257, back] + core[256:257, at] + chip[256:257, at] + other[128:129, 0:128] * weights[t]
        )
    return blocks, rows


def sweep_kernel(flags, scaled, own, core, chip, other, near, message, to_half):
    blocks, rows = beside(flags[0], own, core, chip, other)
    new, new_rows = [], []
    for t in range(2):
        at = slice(t * 128, t * 128 + 128)
        near[at] = blocks[t]
        new.append(dot(scaled[at], blocks[t]))
        message[at] = new[t]
        new_rows.append(dot(rows[t], scaled[at]))
    put_rows(near, *rows)
    put_rows(message, *new_rows)
    put_half(flags[0], to_half, new, new_rows)


def ring_columns(ref, b, count):
    parts = [ref[0:256, ((b + m) % 4) * 128 : ((b + m) % 4) * 128 + 128] for m in range(count)]
    return jnp.concatenate(parts, axis=1)


def gram_early_kernel(pack, coupling, first, own, near, gram, gather):
    for b in range(4):
        count = 3 if b < 2 else 2
        at = slice(b * 128, b * 128 + 128)
        part = dot(coupling[0:256, at], ring_columns(first, b, count), TN)
        part = part + dot(own[0:256, at], ring_columns(near, b, count), TN)
        gram[at, 0 : count * 128] = part
        if count == 2:
            gram[at, 256:384] = jnp.zeros((128, 128), F32)
    row = jnp.zeros((1, 512), F32)
    for t in range(2):
        at = slice(t * 128, t * 128 + 128)
        row = row + dot(pack[256 + t : 257 + t], first[at])
        row = row + dot(near[256:257, at], own[at])
    gather[0:8] = jnp.broadcast_to(row, (8, 512))


def gram_late_kernel(
    flags, gram, gather, right, own0, own2, near1, own2_core, chip, other, near2, keep, send, total, both, fields
):
    blocks, rows = beside(flags[0], own2, own2_core, chip, other)
    both[...] = own0[0:256] + own2[0:256]
    row = gather[0:1]
    for t in range(2):
        at = slice(t * 128, t * 128 + 128)
        near2[at] = blocks[t]
        fields[at] = near1[at] + blocks[t]
        row = row + dot(rows[t] + near1[256:257, at], both[at])
    put_rows(near2, *rows)
    for b in range(4):
        count = 3 if b < 2 else 2
        at = slice(b * 128, b * 128 + 128)
        part = gram[at, 0 : count * 128] + dot(both[0:256, at], ring_columns(fields, b, count), TN)
        for m in range(4):
            for j in range(4):
                source = part[m * 32 + j * 8 : m * 32 + j * 8 + 8]
                total[j % 2, j // 2, b * 32 + m * 8 : b * 32 + m * 8 + 8, 0 : count * 128] = source
                if count == 2:
                    extra = jnp.zeros((8, 128), F32)
                    if b == 2 and m == 0 and j == 0:
                        four = jnp.concatenate([row[:, i * 128 : i * 128 + 128] for i in range(4)], axis=0)
                        extra = jnp.concatenate([four - right[0:4], jnp.zeros((4, 128), F32)], axis=0)
                    total[j % 2, j // 2, b * 32 + m * 8 : b * 32 + m * 8 + 8, 256:384] = extra
    keep[...] = total[flags[1]]
    send[...] = total[1 - flags[1]]


def halve_kernel(flags, mine, theirs, keep, send):
    keep[...] = mine[flags[2]] + theirs[flags[2]]
    send[...] = mine[1 - flags[2]] + theirs[1 - flags[2]]


def parent_kernel(flags, mine, across_x, across_core, root_part, upper, solved, solved_row, held):
    leaf = flags[3]
    held[:, leaf] = mine[...]
    held[:, leaf ^ 2] = across_x[...]
    held[:, leaf ^ 1] = across_core[0]
    held[:, leaf ^ 3] = across_core[1]

    def block(b, m):
        return held[4 * b : 4 * b + 4, :, :, m * 128 : m * 128 + 128].reshape(128, 128)

    entry = {}
    for b in range(4):
        for j in range(b, 4):
            entry[b, j] = block(3, 1).T if (b, j) == (0, 3) else block(b, j - b)
    rhs = [held[4 * b : 4 * b + 4, :, :, 384:640].reshape(128, 256) for b in range(4)]
    reduced = held[8, 0, :, 256:384]
    rows = [reduced[b : b + 1] for b in range(4)]
    part = jnp.zeros((256, 256), F32)
    part_row = jnp.zeros((1, 256), F32)
    upper[...] = jnp.zeros((384, 512), F32)
    for b in range(4):
        (inverse,) = inverses([entry[b, b]])
        wide = jnp.concatenate([entry[b, j] for j in range(b + 1, 4)] + [rhs[b]], axis=1)
        wide = dot(inverse, wide)
        span = (3 - b) * 128
        done = wide[:, span:]
        solved[b * 128 : b * 128 + 128] = done
        row = dot(rows[b], inverse)
        solved_row[0:8, b * 128 : b * 128 + 128] = jnp.broadcast_to(row, (8, 128))
        for i in range(b + 1, 4):
            left = entry[b, i]
            skip = (i - b - 1) * 128
            change = dot(left, wide[:, skip:], TN)
            for j in range(i, 4):
                entry[i, j] = entry[i, j] - change[:, (j - i) * 128 : (j - i) * 128 + 128]
            rhs[i] = rhs[i] - change[:, (4 - i) * 128 :]
            rows[i] = rows[i] - dot(row, left)
            upper[b * 128 : b * 128 + 128, i * 128 : i * 128 + 128] = wide[:, skip : skip + 128]
        part = part + dot(rhs[b], done, TN)
        part_row = part_row + dot(row, rhs[b])
    root_part[0:256] = part
    root_part[256:264] = jnp.broadcast_to(part_row, (8, 256))


def root_kernel(
    flags, mine, theirs, matrix, right, upper, solved, solved_row, pack, coupling, near0, near1, near2, scaled,
    step, parent, source, message, to_half,
):
    total = matrix[...] + (mine[0:256] + theirs[0:256])
    vector = right[0:1] - (mine[256:257] + theirs[256:257])
    side = total[0:128, 128:256]
    (first,) = inverses([total[0:128, 0:128]])
    pushed = dot(first, side)
    (second,) = inverses([total[128:256, 128:256] - dot(side, pushed, TN)])
    head = dot(vector[:, 0:128], first)
    tail = dot(vector[:, 128:256] - dot(head, side), second)
    head = head - dot(tail, pushed, NT)
    root = jnp.concatenate([head, tail], axis=1)
    step[...] = jnp.broadcast_to(root, (8, 256))
    pieces = [None] * 4
    for b in range(3, -1, -1):
        at = slice(b * 128, b * 128 + 128)
        value = solved_row[0:1, at] + dot(root, solved[at], NT)
        for j in range(b + 1, 4):
            value = value - dot(pieces[j], upper[at, j * 128 : j * 128 + 128], NT)
        pieces[b] = value
    whole = jnp.concatenate(pieces, axis=1)
    parent[...] = jnp.broadcast_to(whole, (8, 512))
    source_rows, message_rows = [], []
    for t in range(2):
        at = slice(t * 128, t * 128 + 128)
        last = near2[256:257, at] - dot(whole, near2[at], NT)
        early = near0[256:257, at] + near1[256:257, at] - dot(whole, near0[at] + near1[at], NT)
        weight = pack[258 + t : 259 + t]
        source_rows.append(pack[256 + t : 257 + t] - dot(whole, coupling[at], NT) + weight * (early + last))
        message_rows.append(dot(last, scaled[at]))
    source[...] = jnp.broadcast_to(jnp.concatenate(source_rows, axis=1), (8, 256))
    message[...] = jnp.broadcast_to(jnp.concatenate(message_rows, axis=1), (8, 256))
    other = jnp.where(flags[0] == 0, message_rows[1], message_rows[0])
    to_half[...] = jnp.broadcast_to(other, (8, 128))


def beside_rows(half, own, core, chip, other):
    late = (half == 1).astype(F32)
    weights = (late, 1.0 - late)
    rows = []
    for t in range(2):
        at = slice(t * 128, t * 128 + 128)
        back = slice(128 - t * 128, 256 - t * 128)
        rows.append(own[0:1, back] + core[0:1, at] + chip[0:1, at] + other[0:1] * weights[t])
    return rows


def vector_kernel(flags, pack, scaled, source, own, core, chip, other, new_source, message, to_half):
    rows = beside_rows(flags[0], own, core, chip, other)
    new = []
    for t in range(2):
        at = slice(t * 128, t * 128 + 128)
        new_source[0:8, at] = jnp.broadcast_to(source[0:1, at] + pack[258 + t : 259 + t] * rows[t], (8, 128))
        new.append(dot(rows[t], scaled[at]))
    message[...] = jnp.broadcast_to(jnp.concatenate(new, axis=1), (8, 256))
    to_half[...] = jnp.broadcast_to(jnp.where(flags[0] == 0, new[1], new[0]), (8, 128))


def finish_kernel(flags, pack, inverse, source, own, core, chip, other, out):
    rows = beside_rows(flags[0], own, core, chip, other)
    for t in range(2):
        at = slice(t * 128, t * 128 + 128)
        full = source[0:1, at] + pack[258 + t : 259 + t] * rows[t]
        out[0:8, at] = jnp.broadcast_to(dot(full, inverse[at]), (8, 128))


def neighbours(message, to_half):
    return (
        lax.ppermute(message, AXES, TO_CORE),
        lax.ppermute(message, AXES, TO_CHIP),
        lax.ppermute(to_half, AXES, TO_HALF),
    )


def body(
    coupling, leaf_rhs, conductance, compressor, blocks, parent_of, parent_mat, parent_rhs, link, root_mat, root_rhs
):
    scen = lax.axis_index("scen")
    space = lax.axis_index("space")
    tm = lax.axis_index("tm")
    z = tm * 8 + space
    strip = space * 2 + tm
    quarter = ((z - Z_SHIFT) % 16) // 4
    core = scen % 2
    column = (scen // 2) % 2
    half = column ^ (quarter % 2)
    flags = jnp.stack([half, core, column, scen % 4]).astype(jnp.int32)

    weight = conductance[0] * (1.0 + compressor[0].astype(F32)[..., None]) * 0.5
    pack = jnp.concatenate(
        [
            blocks[0].reshape(256, 128),
            leaf_rhs[0].reshape(2, 128),
            weight.reshape(2, 128),
            jnp.zeros((4, 128), F32),
        ],
        axis=0,
    )
    pack = lax.ppermute(pack, AXES, MOVE_OUT)
    field = lax.ppermute(coupling[0].reshape(256, 512).astype(F32), AXES, MOVE_OUT)

    label = parent_of[0]
    sibling = scen % 4
    row_block = strip // 4
    matrix_rows = lax.dynamic_slice(parent_mat, (label, sibling * 8, 0), (1, 8, 512))[0]
    matrix_rows = lax.dynamic_slice(
        jnp.concatenate([matrix_rows, matrix_rows], axis=1), (0, row_block * 128), (8, 384)
    )
    spare = (row_block >= 2) & (lax.broadcasted_iota(jnp.int32, (8, 384), 1) >= 256)
    matrix_rows = jnp.where(spare, 0.0, matrix_rows)
    link_rows = lax.dynamic_slice(link, (label, sibling * 8, 0), (1, 8, 256))[0]
    right = lax.dynamic_slice(parent_rhs, (label, 0), (1, 32))[0] * (sibling == 0).astype(F32)
    right = lax.dynamic_update_slice(jnp.zeros((512,), F32), right, (strip * 32,)).reshape(4, 128)
    right = jnp.concatenate([right, jnp.zeros((4, 128), F32)], axis=0)

    inverse, scaled, half_scaled = call(invert_kernel, "invert", [(256, 128)] * 3, pack)
    shapes = [(256, 512), (264, 512), (136, 512)]
    first, own0, half0 = call(
        start_kernel, "start", shapes, flags, pack, inverse, half_scaled, field, scalars=1
    )
    shapes = [(264, 512), (264, 512), (136, 512)]
    near0, own1, half1 = call(
        sweep_kernel, "sweep", shapes, flags, scaled, own0, *neighbours(own0, half0), scalars=1
    )
    around1 = neighbours(own1, half1)
    gram, gather = call(
        gram_early_kernel, "gram_early", [(512, 384), (8, 512)], pack, field, first, own0, near0
    )
    near1, own2, half2 = call(
        sweep_kernel, "sweep", shapes, flags, scaled, own1, *around1, scalars=1
    )
    near2, keep, send = call(
        gram_late_kernel,
        "gram_late",
        [(264, 512), (2, 128, 384), (2, 128, 384)],
        flags, gram, gather, right, own0, own2, near1, *neighbours(own2, half2),
        scalars=1,
        scratch=[pltpu.VMEM((2, 2, 128, 384), F32), pltpu.VMEM((256, 512), F32), pltpu.VMEM((256, 512), F32)],
    )

    keep, send = call(
        halve_kernel, "halve", [(128, 384)] * 2, flags, keep, lax.ppermute(send, "scen", flip(1)), scalars=1
    )
    quarter_sum = keep + lax.ppermute(send, "scen", flip(2))
    shares = lax.all_to_all(quarter_sum.reshape(16, 8, 384), Z_AXES, 0, 0)
    share = jnp.concatenate([jnp.sum(shares, axis=0) + matrix_rows, link_rows], axis=1)
    mine = lax.all_to_all(jnp.broadcast_to(share[None], (16, 8, 640)), Z_AXES, 0, 0)
    across_x = lax.ppermute(mine, "scen", flip(2))
    across_core = lax.ppermute(jnp.stack([mine, across_x]), "scen", flip(1))

    part, upper, solved, solved_row = call(
        parent_kernel,
        "parent",
        [(264, 256), (384, 512), (512, 256), (8, 512)],
        flags, mine, across_x, across_core,
        scalars=1,
        scratch=[pltpu.VMEM((16, 4, 8, 640), F32)],
    )
    part = part + lax.ppermute(part, "scen", flip(4))
    part = part + lax.ppermute(part, "scen", flip(8))
    step, parent, source, message, to_half = call(
        root_kernel,
        "root",
        [(8, 256), (8, 512), (8, 256), (8, 256), (8, 128)],
        flags, part, lax.ppermute(part, "scen", flip(16)), root_mat,
        jnp.broadcast_to(root_rhs[None], (8, 256)), upper, solved, solved_row, pack, field, near0, near1, near2, scaled,
        scalars=1,
    )
    source, message, to_half = call(
        vector_kernel,
        "vector",
        [(8, 256), (8, 256), (8, 128)],
        flags, pack, scaled, source, message, *neighbours(message, to_half),
        scalars=1,
    )
    (move,) = call(
        finish_kernel,
        "finish",
        [(8, 256)],
        flags, pack, inverse, source, message, *neighbours(message, to_half),
        scalars=1,
    )
    move = lax.ppermute(move, AXES, MOVE_BACK)
    parent_at_leaf = lax.dynamic_slice(parent, (0, strip * 32), (1, 32))
    return move[0].reshape(1, 2, 1, 128), parent_at_leaf, step[0]


def solution(mesh):
    return jax.shard_map(
        body,
        mesh=mesh,
        in_specs=(
            P("scen", "tm", "space", None, None),
            P("scen", "tm", "space", None),
            P("scen", "tm", "space", None),
            P("scen", "tm", "space"),
            P("scen", "tm", "space", None, None),
            P("scen"),
            P(None, ("space", "tm"), None),
            P(None, ("space", "tm")),
            P(None, ("space", "tm"), None),
            P(),
            P(),
        ),
        out_specs=(P("scen", "tm", "space", None), P("scen", ("space", "tm")), P()),
        check_vma=False,
    )
```

```python
import functools

import jax
import jax.numpy as jnp
from jax import lax
from jax.experimental import pallas as pl
from jax.experimental.pallas import tpu as pltpu
from jax.sharding import PartitionSpec as P

AXES = ("scen", "space", "tm")
Z_AXES = ("space", "tm")
F32 = jnp.float32
HIGH = lax.Precision.HIGHEST

QUARTER = (0, 2, 1, 3)
LEAF_OF_QUARTER = (0, 2, 1, 3)
Z_SHIFT = 2


def linear(scen, z):
    return (scen * 8 + z % 8) * 2 + z // 8


def home(group, leaf, half, cell):
    return linear(group * 4 + leaf, half * 8 + cell)


def away(group, leaf, half, cell):
    column = half ^ (leaf // 2)
    z = (4 * QUARTER[leaf] + 3 - cell // 2 + Z_SHIFT) % 16
    return linear(group * 4 + column * 2 + cell % 2, z)


def every_cell():
    for group in range(8):
        for leaf in range(4):
            for half in range(2):
                for cell in range(8):
                    yield group, leaf, half, cell


MOVE_OUT = [(home(*at), away(*at)) for at in every_cell()]
MOVE_BACK = [(there, here) for here, there in MOVE_OUT]
TO_CORE = [(away(g, l, h, c), away(g, l, h, c ^ 1)) for g, l, h, c in every_cell()]
TO_HALF = [(away(g, l, h, c), away(g, l, h ^ 1, c)) for g, l, h, c in every_cell()]
TO_CHIP = [
    (away(g, l, h, c), away(g, l, h, c + (1 if c % 2 else -1)))
    for g, l, h, c in every_cell()
    if 0 <= c + (1 if c % 2 else -1) < 8
]


def flip(bit):
    return [(i, i ^ bit) for i in range(32)]


def dot(a, b, dims=((1,), (0,)), precision=HIGH):
    return lax.dot_general(a, b, (dims, ((), ())), precision=precision, preferred_element_type=F32)


NT = ((1,), (1,))
TN = ((0,), (0,))


def sweep8(matrix, lane, sub):
    columns = [jnp.broadcast_to(matrix[:, k : k + 1], (128, 128)) for k in range(8)]
    small = [c[:8] for c in columns]
    rows = jnp.where(lane < 8, (sub == lane).astype(F32), matrix[:8])
    for k in range(0, 8, 2):
        a, b, c = small[k][k : k + 1], small[k][k + 1 : k + 2], small[k + 1][k + 1 : k + 2]
        scale = 1.0 / (a * c - b * b)
        a, b, c = a * scale, b * scale, c * scale
        here, after, pair = sub == k, sub == k + 1, (sub == k) | (sub == k + 1)
        left = jnp.where(here, -1.0, jnp.where(after, 0.0, small[k]))
        next_left = jnp.where(after, -1.0, jnp.where(here, 0.0, small[k + 1]))

        def eliminate(panel):
            one, two = panel[k : k + 1], panel[k + 1 : k + 2]
            first = c * one - b * two
            second = a * two - b * one
            return (jnp.where(pair, 0.0, panel) - left * first) - next_left * second

        for j in range(k + 2, 8):
            small[j] = eliminate(small[j])
        rows = eliminate(rows)
    rest = jnp.where(lane < 8, 0.0, matrix[8:])
    for k in range(8):
        rest = rest - columns[k][8:] * rows[k : k + 1]
    return jnp.concatenate([rest, rows], axis=0)


def inverses(matrices):
    lane = lax.broadcasted_iota(jnp.int32, (1, 128), 1)
    sub = lax.broadcasted_iota(jnp.int32, (8, 1), 0)

    def step(_, carry):
        return tuple(pltpu.roll(sweep8(m, lane, sub), 120, 1) for m in carry)

    return lax.fori_loop(0, 16, step, tuple(matrices))


def call(kernel, name, shapes, *operands, scratch=(), scalars=0):
    smem = pl.BlockSpec(memory_space=pltpu.SMEM)
    vmem = pl.BlockSpec(memory_space=pltpu.VMEM)
    return pl.pallas_call(
        kernel,
        name=name,
        out_shape=[jax.ShapeDtypeStruct(s, F32) for s in shapes],
        in_specs=[smem] * scalars + [vmem] * (len(operands) - scalars),
        out_specs=[vmem] * len(shapes),
        scratch_shapes=list(scratch),
    )(*operands)


def invert_kernel(blocks, rows, pack):
    found = inverses([blocks[0:128], blocks[128:256]])
    pack[0:128] = found[0]
    pack[128:256] = found[1]
    pack[256:264] = rows[...]


def put_rows(out, first, second):
    out[256:264] = jnp.zeros((8, 512), F32)
    out[256:257, 0:128] = first
    out[256:257, 128:256] = second


def put_half(half, out, blocks, rows):
    early = half == 0
    out[0:128] = jnp.where(early, blocks[1], blocks[0])
    out[128:136] = jnp.zeros((8, 512), F32)
    out[128:129, 0:128] = jnp.where(early, rows[1], rows[0])


def start_kernel(flags, pack, coupling, first, scaled, message, to_half):
    blocks, rows = [], []
    for t in range(2):
        at = slice(t * 128, t * 128 + 128)
        weight = pack[258 + t : 259 + t]
        across = jnp.broadcast_to(weight, (128, 128))
        down = across.T
        inverse = pack[at]
        scaled[at] = down * inverse * across
        field = dot(inverse, coupling[at])
        first[at] = field
        blocks.append(jnp.concatenate([down] * 4, axis=1) * field)
        message[at] = blocks[t]
        rows.append(dot(pack[256 + t : 257 + t], inverse) * weight)
    put_rows(message, *rows)
    put_half(flags[0], to_half, blocks, rows)


def beside(half, own, core, chip, other):
    late = (half == 1).astype(F32)
    weights = (late, 1.0 - late)
    blocks, rows = [], []
    for t in range(2):
        at = slice(t * 128, t * 128 + 128)
        back = slice(128 - t * 128, 256 - t * 128)
        blocks.append(own[back] + core[at] + chip[at] + other[0:128] * weights[t])
        rows.append(
            own[256:257, back] + core[256:257, at] + chip[256:257, at] + other[128:129, 0:128] * weights[t]
        )
    return blocks, rows


def sweep_kernel(flags, scaled, own, core, chip, other, near, message, to_half):
    blocks, rows = beside(flags[0], own, core, chip, other)
    new, new_rows = [], []
    for t in range(2):
        at = slice(t * 128, t * 128 + 128)
        near[at] = blocks[t]
        new.append(dot(scaled[at], blocks[t]))
        message[at] = new[t]
        new_rows.append(dot(rows[t], scaled[at]))
    put_rows(near, *rows)
    put_rows(message, *new_rows)
    put_half(flags[0], to_half, new, new_rows)


def apply_kernel(flags, scaled, near, message, to_half):
    new, new_rows = [], []
    for t in range(2):
        at = slice(t * 128, t * 128 + 128)
        new.append(dot(scaled[at], near[at]))
        message[at] = new[t]
        new_rows.append(dot(near[256:257, at], scaled[at]))
    put_rows(message, *new_rows)
    put_half(flags[0], to_half, new, new_rows)


def total_kernel(flags, near0, near1, near2, near3, own, core, chip, other, total):
    blocks, rows = beside(flags[0], own, core, chip, other)
    for t in range(2):
        at = slice(t * 128, t * 128 + 128)
        total[at] = ((near0[at] + near1[at]) + (near2[at] + near3[at])) + blocks[t]
        rows[t] = rows[t] + ((near0[256:257, at] + near1[256:257, at]) + (near2[256:257, at] + near3[256:257, at]))
    put_rows(total, *rows)


def leaf_kernel(pack, coupling, total, solved, pulled):
    for t in range(2):
        at = slice(t * 128, t * 128 + 128)
        weight = pack[258 + t : 259 + t]
        down = jnp.broadcast_to(weight, (128, 128)).T
        source = coupling[at].astype(F32) + jnp.concatenate([down] * 4, axis=1) * total[at]
        solved[at] = dot(pack[at], source)
        row = dot(pack[256 + t : 257 + t] + weight * total[256:257, at], pack[at])
        pulled[0:8, at] = jnp.broadcast_to(row, (8, 128))


def ring_columns(ref, b, count):
    parts = [ref[0:256, ((b + m) % 4) * 128 : ((b + m) % 4) * 128 + 128] for m in range(count)]
    return jnp.concatenate(parts, axis=1)


def gram_early_kernel(pack, coupling, first, own, near, gram, gather):
    for b in range(4):
        count = 3 if b < 2 else 2
        at = slice(b * 128, b * 128 + 128)
        part = dot(coupling[0:256, at], ring_columns(first, b, count), TN)
        part = part + dot(own[0:256, at], ring_columns(near, b, count), TN)
        gram[at, 0 : count * 128] = part
        if count == 2:
            gram[at, 256:384] = jnp.zeros((128, 128), F32)
    row = jnp.zeros((1, 512), F32)
    for t in range(2):
        at = slice(t * 128, t * 128 + 128)
        row = row + dot(pack[256 + t : 257 + t], first[at])
        row = row + dot(near[256:257, at], own[at])
    gather[0:8] = jnp.broadcast_to(row, (8, 512))


def gram_late_kernel(
    flags, gram, gather, right, own0, own2, near1, own2_core, chip, other, near2, keep, send, total, both, fields
):
    blocks, rows = beside(flags[0], own2, own2_core, chip, other)
    both[...] = own0[0:256] + own2[0:256]
    row = gather[0:1]
    for t in range(2):
        at = slice(t * 128, t * 128 + 128)
        near2[at] = blocks[t]
        fields[at] = near1[at] + blocks[t]
        row = row + dot(rows[t] + near1[256:257, at], both[at])
    put_rows(near2, *rows)
    for b in range(4):
        count = 3 if b < 2 else 2
        at = slice(b * 128, b * 128 + 128)
        part = gram[at, 0 : count * 128] + dot(both[0:256, at], ring_columns(fields, b, count), TN)
        for m in range(4):
            for j in range(4):
                source = part[m * 32 + j * 8 : m * 32 + j * 8 + 8]
                total[j % 2, j // 2, b * 32 + m * 8 : b * 32 + m * 8 + 8, 0 : count * 128] = source
                if count == 2:
                    extra = jnp.zeros((8, 128), F32)
                    if b == 2 and m == 0 and j == 0:
                        four = jnp.concatenate([row[:, i * 128 : i * 128 + 128] for i in range(4)], axis=0)
                        extra = jnp.concatenate([four - right[0:4], jnp.zeros((4, 128), F32)], axis=0)
                    total[j % 2, j // 2, b * 32 + m * 8 : b * 32 + m * 8 + 8, 256:384] = extra
    keep[...] = total[flags[1]]
    send[...] = total[1 - flags[1]]


def halve_kernel(flags, mine, theirs, keep, send):
    keep[...] = mine[flags[2]] + theirs[flags[2]]
    send[...] = mine[1 - flags[2]] + theirs[1 - flags[2]]


def parent_kernel(flags, mine, across_x, across_core, root_part, upper, solved, solved_row, held):
    leaf = flags[3]
    held[:, leaf] = mine[...]
    held[:, leaf ^ 2] = across_x[...]
    held[:, leaf ^ 1] = across_core[0]
    held[:, leaf ^ 3] = across_core[1]

    def block(b, m):
        return held[4 * b : 4 * b + 4, :, :, m * 128 : m * 128 + 128].reshape(128, 128)

    entry = {}
    for b in range(4):
        for j in range(b, 4):
            entry[b, j] = block(3, 1).T if (b, j) == (0, 3) else block(b, j - b)
    rhs = [held[4 * b : 4 * b + 4, :, :, 384:640].reshape(128, 256) for b in range(4)]
    reduced = held[8, 0, :, 256:384]
    rows = [reduced[b : b + 1] for b in range(4)]
    part = jnp.zeros((256, 256), F32)
    part_row = jnp.zeros((1, 256), F32)
    upper[...] = jnp.zeros((384, 512), F32)
    for b in range(4):
        (inverse,) = inverses([entry[b, b]])
        wide = jnp.concatenate([entry[b, j] for j in range(b + 1, 4)] + [rhs[b]], axis=1)
        wide = dot(inverse, wide)
        span = (3 - b) * 128
        done = wide[:, span:]
        solved[b * 128 : b * 128 + 128] = done
        row = dot(rows[b], inverse)
        solved_row[0:8, b * 128 : b * 128 + 128] = jnp.broadcast_to(row, (8, 128))
        for i in range(b + 1, 4):
            left = entry[b, i]
            skip = (i - b - 1) * 128
            change = dot(left, wide[:, skip:], TN)
            for j in range(i, 4):
                entry[i, j] = entry[i, j] - change[:, (j - i) * 128 : (j - i) * 128 + 128]
            rhs[i] = rhs[i] - change[:, (4 - i) * 128 :]
            rows[i] = rows[i] - dot(row, left)
            upper[b * 128 : b * 128 + 128, i * 128 : i * 128 + 128] = wide[:, skip : skip + 128]
        part = part + dot(rhs[b], done, TN)
        part_row = part_row + dot(row, rhs[b])
    root_part[0:128] = part[0:128, 0:128]
    root_part[128:256] = part[0:128, 128:256]
    root_part[256:384] = part[128:256, 128:256]
    root_part[384:388] = jnp.broadcast_to(part_row[:, 0:128], (4, 128))
    root_part[388:392] = jnp.broadcast_to(part_row[:, 128:256], (4, 128))


def root_kernel(
    flags, mine, opposite, below, above, matrix, right, upper, solved, solved_row, leaf_solved, pulled, step, parent, move,
):
    part = (mine[...] + opposite[...]) + (below[...] + above[...])
    side = matrix[0:128, 128:256] + part[128:256]
    (first,) = inverses([matrix[0:128, 0:128] + part[0:128]])
    pushed = dot(first, side)
    (second,) = inverses([matrix[128:256, 128:256] + part[256:384] - dot(side, pushed, TN)])
    head = dot(right[0:1, 0:128] - part[384:385], first)
    tail = dot(right[0:1, 128:256] - part[388:389] - dot(head, side), second)
    head = head - dot(tail, pushed, NT)
    root = jnp.concatenate([head, tail], axis=1)
    step[...] = root
    pieces = [None] * 4
    for b in range(3, -1, -1):
        at = slice(b * 128, b * 128 + 128)
        value = solved_row[0:1, at] + dot(root, solved[at], NT)
        for j in range(b + 1, 4):
            value = value - dot(pieces[j], upper[at, j * 128 : j * 128 + 128], NT)
        pieces[b] = value
    chosen = jnp.zeros((1, 128), F32)
    for b in range(4):
        chosen = chosen + jnp.where(flags[4] == b, pieces[b], 0.0)
    chosen = pltpu.roll(jnp.broadcast_to(chosen, (8, 128)), flags[5], 1)
    parent[...] = chosen[0:1, 0:32]
    whole = jnp.concatenate(pieces, axis=1)
    for t in range(2):
        at = slice(t * 128, t * 128 + 128)
        move[t : t + 1] = pulled[0:1, at] - dot(whole, leaf_solved[at], NT)


def neighbours(message, to_half):
    return (
        lax.ppermute(message, AXES, TO_CORE),
        lax.ppermute(message, AXES, TO_CHIP),
        lax.ppermute(to_half, AXES, TO_HALF),
    )


def body(
    coupling, leaf_rhs, conductance, compressor, blocks, parent_of, parent_mat, parent_rhs, link, root_mat, root_rhs
):
    scen = lax.axis_index("scen")
    space = lax.axis_index("space")
    tm = lax.axis_index("tm")
    z = tm * 8 + space
    strip = space * 2 + tm
    quarter = ((z - Z_SHIFT) % 16) // 4
    core = scen % 2
    column = (scen // 2) % 2
    half = column ^ (quarter % 2)
    turn = (128 - (strip % 4) * 32) % 128
    flags = jnp.stack([half, core, column, scen % 4, strip // 4, turn]).astype(jnp.int32)

    weight = conductance[0] * (1.0 + compressor[0].astype(F32)[..., None]) * 0.5
    own_coupling = coupling[0].reshape(256, 512)
    rows = jnp.concatenate(
        [leaf_rhs[0].reshape(2, 128), weight.reshape(2, 128), jnp.zeros((4, 128), F32)], axis=0
    )
    field = lax.ppermute(own_coupling.astype(F32), AXES, MOVE_OUT)
    (own_pack,) = call(invert_kernel, "invert", [(264, 128)], blocks[0].reshape(256, 128), rows)
    pack = lax.ppermute(own_pack, AXES, MOVE_OUT)

    label = parent_of[0]
    sibling = scen % 4
    row_block = strip // 4
    matrix_rows = lax.dynamic_slice(parent_mat, (label, sibling * 8, 0), (1, 8, 512))[0]
    matrix_rows = lax.dynamic_slice(
        jnp.concatenate([matrix_rows, matrix_rows], axis=1), (0, row_block * 128), (8, 384)
    )
    spare = (row_block >= 2) & (lax.broadcasted_iota(jnp.int32, (8, 384), 1) >= 256)
    matrix_rows = jnp.where(spare, 0.0, matrix_rows)
    link_rows = lax.dynamic_slice(link, (label, sibling * 8, 0), (1, 8, 256))[0]
    right = lax.dynamic_slice(parent_rhs, (label, 0), (1, 32))[0] * (sibling == 0).astype(F32)
    right = lax.dynamic_update_slice(jnp.zeros((512,), F32), right, (strip * 32,)).reshape(4, 128)
    right = jnp.concatenate([right, jnp.zeros((4, 128), F32)], axis=0)

    shapes = [(256, 512), (256, 128), (264, 512), (136, 512)]
    first, scaled, own0, half0 = call(start_kernel, "start", shapes, flags, pack, field, scalars=1)
    shapes = [(264, 512), (264, 512), (136, 512)]
    near0, own1, half1 = call(
        sweep_kernel, "sweep", shapes, flags, scaled, own0, *neighbours(own0, half0), scalars=1
    )
    around1 = neighbours(own1, half1)
    gram, gather = call(
        gram_early_kernel, "gram_early", [(512, 384), (8, 512)], pack, field, first, own0, near0
    )
    near1, own2, half2 = call(
        sweep_kernel, "sweep", shapes, flags, scaled, own1, *around1, scalars=1
    )
    near2, keep, send = call(
        gram_late_kernel,
        "gram_late",
        [(264, 512), (2, 128, 384), (2, 128, 384)],
        flags, gram, gather, right, own0, own2, near1, *neighbours(own2, half2),
        scalars=1,
        scratch=[pltpu.VMEM((2, 2, 128, 384), F32), pltpu.VMEM((256, 512), F32), pltpu.VMEM((256, 512), F32)],
    )
    own3, half3 = call(apply_kernel, "apply", shapes[1:], flags, scaled, near2, scalars=1)
    around3 = neighbours(own3, half3)
    theirs, _ = lax.optimization_barrier((lax.ppermute(send, "scen", flip(1)), own3))
    keep, send = call(halve_kernel, "halve", [(128, 384)] * 2, flags, keep, theirs, scalars=1)
    quarter_sum = keep + lax.ppermute(send, "scen", flip(2))
    shares = lax.all_to_all(quarter_sum.reshape(16, 8, 384), Z_AXES, 0, 0)
    near3, own4, half4 = call(sweep_kernel, "sweep", shapes, flags, scaled, own3, *around3, scalars=1)
    around4 = neighbours(own4, half4)
    shares, _ = lax.optimization_barrier((shares, own4))
    share = jnp.concatenate([jnp.sum(shares, axis=0) + matrix_rows, link_rows], axis=1)
    mine = lax.all_to_all(jnp.broadcast_to(share[None], (16, 8, 640)), Z_AXES, 0, 0)
    (total,) = call(
        total_kernel, "total", [(264, 512)], flags, near0, near1, near2, near3, own4, *around4, scalars=1
    )
    mine, total = lax.optimization_barrier((mine, total))
    across_x = lax.ppermute(mine, "scen", flip(2))
    across_core = lax.ppermute(jnp.stack([mine, across_x]), "scen", flip(1))

    total = lax.ppermute(total, AXES, MOVE_BACK)
    leaf_solved, pulled = call(leaf_kernel, "leaf", [(256, 512), (8, 256)], own_pack, own_coupling, total)

    part, upper, solved, solved_row = call(
        parent_kernel,
        "parent",
        [(392, 128), (384, 512), (512, 256), (8, 512)],
        flags, mine, across_x, across_core,
        scalars=1,
        scratch=[pltpu.VMEM((16, 4, 8, 640), F32)],
    )
    part = part + lax.ppermute(part, "scen", flip(4))
    others = [lax.ppermute(part, "scen", [(i, (i + by) % 32) for i in range(32)]) for by in (16, 8, 24)]
    step, parent, move = call(
        root_kernel,
        "root",
        [(1, 256), (1, 32), (2, 128)],
        flags, part, *others, root_mat, root_rhs.reshape(1, 256), upper, solved, solved_row, leaf_solved, pulled,
        scalars=1,
    )
    return move.reshape(1, 2, 1, 128), parent, step.reshape(256)


def solution(mesh):
    return jax.shard_map(
        body,
        mesh=mesh,
        in_specs=(
            P("scen", "tm", "space", None, None),
            P("scen", "tm", "space", None),
            P("scen", "tm", "space", None),
            P("scen", "tm", "space"),
            P("scen", "tm", "space", None, None),
            P("scen"),
            P(None, ("space", "tm"), None),
            P(None, ("space", "tm")),
            P(None, ("space", "tm"), None),
            P(),
            P(),
        ),
        out_specs=(P("scen", "tm", "space", None), P("scen", ("space", "tm")), P()),
        check_vma=False,
    )
```

```python
import functools

import jax
import jax.numpy as jnp
from jax import lax
from jax.experimental import pallas as pl
from jax.experimental.pallas import tpu as pltpu
from jax.sharding import PartitionSpec as P

AXES = ("scen", "space", "tm")
Z_AXES = ("space", "tm")
F32 = jnp.float32
HIGH = lax.Precision.HIGHEST

QUARTER = (0, 2, 1, 3)
Z_SHIFT = 2


def linear(scen, z):
    return (scen * 8 + z % 8) * 2 + z // 8


def home(group, leaf, half, cell):
    return linear(group * 4 + leaf, half * 8 + cell)


def away(group, leaf, half, cell):
    column = half ^ (leaf // 2)
    z = (4 * QUARTER[leaf] + 3 - cell // 2 + Z_SHIFT) % 16
    return linear(group * 4 + column * 2 + cell % 2, z)


def every_cell():
    for group in range(8):
        for leaf in range(4):
            for half in range(2):
                for cell in range(8):
                    yield group, leaf, half, cell


MOVE_OUT = [(home(*at), away(*at)) for at in every_cell()]
MOVE_BACK = [(there, here) for here, there in MOVE_OUT]
TO_CORE = [(away(g, l, h, c), away(g, l, h, c ^ 1)) for g, l, h, c in every_cell()]
TO_HALF = [(away(g, l, h, c), away(g, l, h ^ 1, c)) for g, l, h, c in every_cell()]
TO_CHIP = [
    (away(g, l, h, c), away(g, l, h, c + (1 if c % 2 else -1)))
    for g, l, h, c in every_cell()
    if 0 <= c + (1 if c % 2 else -1) < 8
]


SAME_CORE = [
    [((group * 4 + column * 2 + core) * 8 + space) * 2 + tm for column in range(2) for space in range(8) for tm in range(2)]
    for group in range(8)
    for core in range(2)
]


def flip(bit):
    return [(i, i ^ bit) for i in range(32)]


def dot(a, b, dims=((1,), (0,)), precision=HIGH):
    return lax.dot_general(a, b, (dims, ((), ())), precision=precision, preferred_element_type=F32)


NT = ((1,), (1,))
TN = ((0,), (0,))


def split(x):
    high = x.astype(jnp.bfloat16)
    return high, (x - high.astype(F32)).astype(jnp.bfloat16)


def dot3(a, b, dims=((1,), (0,))):
    (k,), (m,) = dims
    a_high, a_low = split(a)
    b_high, b_low = split(b)
    plain = functools.partial(
        lax.dot_general, dimension_numbers=(dims, ((), ())), preferred_element_type=F32
    )
    if a.shape[k] < 256:
        first = plain(jnp.concatenate([a_high, a_low], axis=k), jnp.concatenate([b_high, b_high], axis=m))
    else:
        first = plain(a_high, b_high) + plain(a_low, b_high)
    return first + plain(a_high, b_low)


def eliminate(matrix, start, lane, sub):
    stop = start + 16
    inside = (lane >= start) & (lane < stop)
    panel = matrix[start:stop]
    small = [jnp.broadcast_to(panel[:, start + k : start + k + 1], (16, 128)) for k in range(16)]
    rows = jnp.where(inside, (sub == lane - start).astype(F32), panel)
    left = jnp.where(inside, matrix, 0.0)
    for k in range(16):
        scale = 1.0 / small[k][k : k + 1]
        factor = jnp.where(sub == k, -1.0, small[k])

        def step(block):
            return jnp.where(sub == k, 0.0, block) - factor * (block[k : k + 1] * scale)

        for j in range(k + 1, 16):
            small[j] = step(small[j])
        rows = step(rows)
    spread = [jnp.zeros((n, 128), F32) for n in (start, 112 - start) if n]
    spread.insert(1 if start else 0, rows)
    rest = jnp.where(inside, 0.0, matrix) - dot(left, jnp.concatenate(spread, axis=0))
    kept = [rest[stop:]] if stop < 128 else []
    return jnp.concatenate(([rest[:start]] if start else []) + [rows] + kept, axis=0)


def inverses(matrices):
    lane = lax.broadcasted_iota(jnp.int32, (1, 128), 1)
    sub = lax.broadcasted_iota(jnp.int32, (16, 1), 0)

    def step(_, carry):
        out = [eliminate(eliminate(m, 0, lane, sub), 16, lane, sub) for m in carry]
        return tuple(pltpu.roll(jnp.concatenate([m[32:], m[:32]], axis=0), 96, 1) for m in out)

    return lax.fori_loop(0, 4, step, tuple(matrices))


def call(kernel, shapes, *operands, scratch=(), scalars=0):
    smem = pl.BlockSpec(memory_space=pltpu.SMEM)
    vmem = pl.BlockSpec(memory_space=pltpu.VMEM)
    return pl.pallas_call(
        kernel,
        out_shape=[jax.ShapeDtypeStruct(s, F32) for s in shapes],
        in_specs=[smem] * scalars + [vmem] * (len(operands) - scalars),
        out_specs=[vmem] * len(shapes),
        scratch_shapes=list(scratch),
    )(*operands)


def triangles():
    row = lax.broadcasted_iota(jnp.int32, (128, 128), 0)
    column = lax.broadcasted_iota(jnp.int32, (128, 128), 1)
    return row, column


def invert_kernel(blocks, rows, inverse, pack):
    found = inverses([blocks[0:128], blocks[128:256]])
    inverse[0:128] = found[0]
    inverse[128:256] = found[1]
    row, column = triangles()
    pack[0:128] = jnp.where(row >= column, found[0], found[1])
    pack[128:136] = rows[...]
    pack[132:133] = jnp.sum(jnp.where(row == column, found[1], 0.0), axis=0, keepdims=True)


def put_rows(out, first, second):
    out[256:264] = jnp.zeros((8, 512), F32)
    out[256:257, 0:128] = first
    out[256:257, 128:256] = second


def put_half(half, out, blocks, rows):
    early = half == 0
    out[0:128] = jnp.where(early, blocks[1], blocks[0])
    out[128:136] = jnp.zeros((8, 512), F32)
    out[128:129, 0:128] = jnp.where(early, rows[1], rows[0])


def start_kernel(flags, pack, coupling, first, scaled, message, to_half):
    row, column = triangles()
    packed = pack[0:128]
    turned = packed.T
    diagonal = jnp.broadcast_to(pack[132:133], (128, 128))
    inverses_here = [
        jnp.where(row >= column, packed, turned),
        jnp.where(row < column, packed, jnp.where(row > column, turned, diagonal)),
    ]
    blocks, rows = [], []
    for t in range(2):
        at = slice(t * 128, t * 128 + 128)
        weight = pack[130 + t : 131 + t]
        across = jnp.broadcast_to(weight, (128, 128))
        down = across.T
        inverse = inverses_here[t]
        scaled[at] = down * inverse * across
        field = dot3(inverse, coupling[at])
        first[at] = field
        blocks.append(jnp.concatenate([down] * 4, axis=1) * field)
        message[at] = blocks[t]
        rows.append(dot(pack[128 + t : 129 + t], inverse) * weight)
    put_rows(message, *rows)
    put_half(flags[0], to_half, blocks, rows)


def beside(half, own, core, chip, other):
    late = (half == 1).astype(F32)
    weights = (late, 1.0 - late)
    blocks, rows = [], []
    for t in range(2):
        at = slice(t * 128, t * 128 + 128)
        back = slice(128 - t * 128, 256 - t * 128)
        blocks.append(own[back] + core[at] + chip[at] + other[0:128] * weights[t])
        rows.append(
            own[256:257, back] + core[256:257, at] + chip[256:257, at] + other[128:129, 0:128] * weights[t]
        )
    return blocks, rows


def sweep_kernel(flags, scaled, own, core, chip, other, near, message, to_half):
    blocks, rows = beside(flags[0], own, core, chip, other)
    new, new_rows = [], []
    for t in range(2):
        at = slice(t * 128, t * 128 + 128)
        near[at] = blocks[t]
        new.append(dot3(scaled[at], blocks[t]))
        message[at] = new[t]
        new_rows.append(dot(rows[t], scaled[at]))
    put_rows(near, *rows)
    put_rows(message, *new_rows)
    put_half(flags[0], to_half, new, new_rows)


def apply_kernel(flags, scaled, near, message, to_half):
    new, new_rows = [], []
    for t in range(2):
        at = slice(t * 128, t * 128 + 128)
        new.append(dot3(scaled[at], near[at]))
        message[at] = new[t]
        new_rows.append(dot(near[256:257, at], scaled[at]))
    put_rows(message, *new_rows)
    put_half(flags[0], to_half, new, new_rows)


def total_kernel(flags, near0, near1, near2, near3, own, core, chip, other, total):
    blocks, rows = beside(flags[0], own, core, chip, other)
    for t in range(2):
        at = slice(t * 128, t * 128 + 128)
        total[at] = ((near0[at] + near1[at]) + (near2[at] + near3[at])) + blocks[t]
        rows[t] = rows[t] + ((near0[256:257, at] + near1[256:257, at]) + (near2[256:257, at] + near3[256:257, at]))
    put_rows(total, *rows)


def leaf_kernel(inverse, rows, coupling, total, solved, pulled):
    for t in range(2):
        at = slice(t * 128, t * 128 + 128)
        weight = rows[2 + t : 3 + t]
        down = jnp.broadcast_to(weight, (128, 128)).T
        source = coupling[at].astype(F32) + jnp.concatenate([down] * 4, axis=1) * total[at]
        solved[at] = dot3(inverse[at], source)
        row = dot(rows[t : t + 1] + weight * total[256:257, at], inverse[at])
        pulled[0:8, at] = jnp.broadcast_to(row, (8, 128))


def ring_columns(ref, b, count):
    parts = [ref[0:256, ((b + m) % 4) * 128 : ((b + m) % 4) * 128 + 128] for m in range(count)]
    return jnp.concatenate(parts, axis=1)


def gram_early_kernel(pack, coupling, first, own, near, gram, gather):
    for b in range(4):
        count = 3 if b < 2 else 2
        at = slice(b * 128, b * 128 + 128)
        part = dot3(coupling[0:256, at], ring_columns(first, b, count), TN)
        part = part + dot3(own[0:256, at], ring_columns(near, b, count), TN)
        gram[at, 0 : count * 128] = part
        if count == 2:
            gram[at, 256:384] = jnp.zeros((128, 128), F32)
    row = jnp.zeros((1, 512), F32)
    for t in range(2):
        at = slice(t * 128, t * 128 + 128)
        row = row + dot(pack[128 + t : 129 + t], first[at])
        row = row + dot(near[256:257, at], own[at])
    gather[0:8] = jnp.broadcast_to(row, (8, 512))


def gram_late_kernel(
    flags, gram, gather, right, own0, own2, near1, own2_core, chip, other, near2, keep, send, total, both, fields
):
    blocks, rows = beside(flags[0], own2, own2_core, chip, other)
    both[...] = own0[0:256] + own2[0:256]
    row = gather[0:1]
    for t in range(2):
        at = slice(t * 128, t * 128 + 128)
        near2[at] = blocks[t]
        fields[at] = near1[at] + blocks[t]
        row = row + dot(rows[t] + near1[256:257, at], both[at])
    put_rows(near2, *rows)
    for b in range(4):
        count = 3 if b < 2 else 2
        at = slice(b * 128, b * 128 + 128)
        part = gram[at, 0 : count * 128] + dot3(both[0:256, at], ring_columns(fields, b, count), TN)
        for m in range(4):
            for j in range(4):
                source = part[m * 32 + j * 8 : m * 32 + j * 8 + 8]
                total[j % 2, j // 2, b * 32 + m * 8 : b * 32 + m * 8 + 8, 0 : count * 128] = source
                if count == 2:
                    extra = jnp.zeros((8, 128), F32)
                    if b == 2 and m == 0 and j == 0:
                        four = jnp.concatenate([row[:, i * 128 : i * 128 + 128] for i in range(4)], axis=0)
                        extra = jnp.concatenate([four - right[0:4], jnp.zeros((4, 128), F32)], axis=0)
                    total[j % 2, j // 2, b * 32 + m * 8 : b * 32 + m * 8 + 8, 256:384] = extra
    keep[...] = total[flags[1]]
    send[...] = total[1 - flags[1]]


def parent_kernel(
    flags, mine, across_x, across_core, across_both, root_part, upper, solved, solved_row, held
):
    leaf = flags[2]
    held[:, leaf] = mine[...]
    held[:, leaf ^ 2] = across_x[...]
    held[:, leaf ^ 1] = across_core[...]
    held[:, leaf ^ 3] = across_both[...]

    def block(b, m):
        return held[4 * b : 4 * b + 4, :, :, m * 128 : m * 128 + 128].reshape(128, 128)

    entry = {}
    for b in range(4):
        for j in range(b, 4):
            entry[b, j] = block(3, 1).T if (b, j) == (0, 3) else block(b, j - b)
    rhs = [held[4 * b : 4 * b + 4, :, :, 384:640].reshape(128, 256) for b in range(4)]
    reduced = held[8, 0, :, 256:384]
    rows = [reduced[b : b + 1] for b in range(4)]
    part = jnp.zeros((256, 256), F32)
    part_row = jnp.zeros((1, 256), F32)
    upper[...] = jnp.zeros((384, 512), F32)
    for b in range(4):
        (inverse,) = inverses([entry[b, b]])
        wide = jnp.concatenate([entry[b, j] for j in range(b + 1, 4)] + [rhs[b]], axis=1)
        wide = dot(inverse, wide)
        span = (3 - b) * 128
        done = wide[:, span:]
        solved[b * 128 : b * 128 + 128] = done
        row = dot(rows[b], inverse)
        solved_row[0:8, b * 128 : b * 128 + 128] = jnp.broadcast_to(row, (8, 128))
        for i in range(b + 1, 4):
            left = entry[b, i]
            skip = (i - b - 1) * 128
            change = dot(left, wide[:, skip:], TN)
            for j in range(i, 4):
                entry[i, j] = entry[i, j] - change[:, (j - i) * 128 : (j - i) * 128 + 128]
            rhs[i] = rhs[i] - change[:, (4 - i) * 128 :]
            rows[i] = rows[i] - dot(row, left)
            upper[b * 128 : b * 128 + 128, i * 128 : i * 128 + 128] = wide[:, skip : skip + 128]
        part = part + dot(rhs[b], done, TN)
        part_row = part_row + dot(row, rhs[b])
    root_part[0:128] = part[0:128, 0:128]
    root_part[128:256] = part[0:128, 128:256]
    root_part[256:384] = part[128:256, 128:256]
    root_part[384:388] = jnp.broadcast_to(part_row[:, 0:128], (4, 128))
    root_part[388:392] = jnp.broadcast_to(part_row[:, 128:256], (4, 128))


def root_kernel(
    flags, mine, opposite, below, above, matrix, right, upper, solved, solved_row, leaf_solved, pulled, step, parent, move,
):
    part = (mine[...] + opposite[...]) + (below[...] + above[...])
    side = matrix[0:128, 128:256] + part[128:256]
    (first,) = inverses([matrix[0:128, 0:128] + part[0:128]])
    pushed = dot(first, side)
    (second,) = inverses([matrix[128:256, 128:256] + part[256:384] - dot(side, pushed, TN)])
    head = dot(right[0:1, 0:128] - part[384:385], first)
    tail = dot(right[0:1, 128:256] - part[388:389] - dot(head, side), second)
    head = head - dot(tail, pushed, NT)
    root = jnp.concatenate([head, tail], axis=1)
    step[...] = root
    pieces = [None] * 4
    for b in range(3, -1, -1):
        at = slice(b * 128, b * 128 + 128)
        value = solved_row[0:1, at] + dot(root, solved[at], NT)
        for j in range(b + 1, 4):
            value = value - dot(pieces[j], upper[at, j * 128 : j * 128 + 128], NT)
        pieces[b] = value
    chosen = jnp.zeros((1, 128), F32)
    for b in range(4):
        chosen = chosen + jnp.where(flags[3] == b, pieces[b], 0.0)
    chosen = pltpu.roll(jnp.broadcast_to(chosen, (8, 128)), flags[4], 1)
    parent[...] = chosen[0:1, 0:32]
    whole = jnp.concatenate(pieces, axis=1)
    for t in range(2):
        at = slice(t * 128, t * 128 + 128)
        move[t : t + 1] = pulled[0:1, at] - dot(whole, leaf_solved[at], NT)


def neighbours(message, to_half):
    chip = lax.ppermute(message, AXES, TO_CHIP)
    other = lax.ppermute(to_half, AXES, TO_HALF)
    return lax.ppermute(message, AXES, TO_CORE), chip, other


def body(
    coupling, leaf_rhs, conductance, compressor, blocks, parent_of, parent_mat, parent_rhs, link, root_mat, root_rhs
):
    scen = lax.axis_index("scen")
    space = lax.axis_index("space")
    tm = lax.axis_index("tm")
    z = tm * 8 + space
    strip = space * 2 + tm
    quarter = ((z - Z_SHIFT) % 16) // 4
    core = scen % 2
    column = (scen // 2) % 2
    half = column ^ (quarter % 2)
    turn = (128 - (strip % 4) * 32) % 128
    flags = jnp.stack([half, core, scen % 4, strip // 4, turn]).astype(jnp.int32)

    weight = conductance[0] * (1.0 + compressor[0].astype(F32)[..., None]) * 0.5
    own_coupling = coupling[0].reshape(256, 512)
    rows = jnp.concatenate(
        [leaf_rhs[0].reshape(2, 128), weight.reshape(2, 128), jnp.zeros((4, 128), F32)], axis=0
    )
    field = lax.ppermute(own_coupling.astype(F32), AXES, MOVE_OUT)
    own_inverse, own_pack = call(invert_kernel, [(256, 128), (136, 128)], blocks[0].reshape(256, 128), rows)
    pack = lax.ppermute(own_pack, AXES, MOVE_OUT)

    label = parent_of[0]
    sibling = scen % 4
    row_block = strip // 4
    matrix_rows = lax.dynamic_slice(parent_mat, (label, sibling * 8, 0), (1, 8, 512))[0]
    matrix_rows = lax.dynamic_slice(
        jnp.concatenate([matrix_rows, matrix_rows], axis=1), (0, row_block * 128), (8, 384)
    )
    spare = (row_block >= 2) & (lax.broadcasted_iota(jnp.int32, (8, 384), 1) >= 256)
    matrix_rows = jnp.where(spare, 0.0, matrix_rows)
    link_rows = lax.dynamic_slice(link, (label, sibling * 8, 0), (1, 8, 256))[0]
    right = lax.dynamic_slice(parent_rhs, (label, 0), (1, 32))[0] * (sibling == 0).astype(F32)
    right = lax.dynamic_update_slice(jnp.zeros((512,), F32), right, (strip * 32,)).reshape(4, 128)
    right = jnp.concatenate([right, jnp.zeros((4, 128), F32)], axis=0)

    shapes = [(256, 512), (256, 128), (264, 512), (136, 512)]
    first, scaled, own0, half0 = call(start_kernel, shapes, flags, pack, field, scalars=1)
    shapes = [(264, 512), (264, 512), (136, 512)]
    near0, own1, half1 = call(sweep_kernel, shapes, flags, scaled, own0, *neighbours(own0, half0), scalars=1)
    around1 = neighbours(own1, half1)
    gram, gather = call(gram_early_kernel, [(512, 384), (8, 512)], pack, field, first, own0, near0)
    near1, own2, half2 = call(sweep_kernel, shapes, flags, scaled, own1, *around1, scalars=1)
    near2, keep, send = call(
        gram_late_kernel,
        [(264, 512), (2, 128, 384), (2, 128, 384)],
        flags, gram, gather, right, own0, own2, near1, *neighbours(own2, half2),
        scalars=1,
        scratch=[pltpu.VMEM((2, 2, 128, 384), F32), pltpu.VMEM((256, 512), F32), pltpu.VMEM((256, 512), F32)],
    )
    own3, half3 = call(apply_kernel, shapes[1:], flags, scaled, near2, scalars=1)
    around3 = neighbours(own3, half3)
    theirs, _ = lax.optimization_barrier((lax.ppermute(send, "scen", flip(1)), own3))
    half_sum = (keep + theirs).reshape(32, 8, 384)
    shares = lax.all_to_all(half_sum, AXES, 0, 0, axis_index_groups=SAME_CORE)
    near3, own4, half4 = call(sweep_kernel, shapes, flags, scaled, own3, *around3, scalars=1)
    around4 = neighbours(own4, half4)
    shares, _ = lax.optimization_barrier((shares, own4))
    share = jnp.concatenate([jnp.sum(shares, axis=0) + matrix_rows, link_rows], axis=1)
    mine = lax.all_to_all(jnp.broadcast_to(share[None], (16, 8, 640)), Z_AXES, 0, 0)
    (total,) = call(total_kernel, [(264, 512)], flags, near0, near1, near2, near3, own4, *around4, scalars=1)
    mine, total = lax.optimization_barrier((mine, total))
    across_x = lax.ppermute(mine, "scen", flip(2))
    across_core = lax.ppermute(mine, "scen", flip(1))
    across_both = lax.ppermute(across_x, "scen", flip(1))

    total = lax.ppermute(total, AXES, MOVE_BACK)
    leaf_solved, pulled = call(leaf_kernel, [(256, 512), (8, 256)], own_inverse, rows, own_coupling, total)

    part, upper, solved, solved_row = call(
        parent_kernel,
        [(392, 128), (384, 512), (512, 256), (8, 512)],
        flags, mine, across_x, across_core, across_both,
        scalars=1,
        scratch=[pltpu.VMEM((16, 4, 8, 640), F32)],
    )
    part = part + lax.ppermute(part, "scen", flip(4))
    others = [lax.ppermute(part, "scen", [(i, (i + by) % 32) for i in range(32)]) for by in (16, 8, 24)]
    step, parent, move = call(
        root_kernel,
        [(1, 256), (1, 32), (2, 128)],
        flags, part, *others, root_mat, root_rhs.reshape(1, 256), upper, solved, solved_row, leaf_solved, pulled,
        scalars=1,
    )
    return move.reshape(1, 2, 1, 128), parent, step.reshape(256)


def solution(mesh):
    return jax.shard_map(
        body,
        mesh=mesh,
        in_specs=(
            P("scen", "tm", "space", None, None),
            P("scen", "tm", "space", None),
            P("scen", "tm", "space", None),
            P("scen", "tm", "space"),
            P("scen", "tm", "space", None, None),
            P("scen"),
            P(None, ("space", "tm"), None),
            P(None, ("space", "tm")),
            P(None, ("space", "tm"), None),
            P(),
            P(),
        ),
        out_specs=(P("scen", "tm", "space", None), P("scen", ("space", "tm")), P()),
        check_vma=False,
    )
```

```python
import functools

import jax
import jax.numpy as jnp
from jax import lax
from jax.experimental import pallas as pl
from jax.experimental.pallas import tpu as pltpu
from jax.sharding import PartitionSpec as P

AXES = ("scen", "space", "tm")
Z_AXES = ("space", "tm")
F32 = jnp.float32
HIGH = lax.Precision.HIGHEST

QUARTER = (0, 2, 1, 3)
Z_SHIFT = 2


def linear(scen, z):
    return (scen * 8 + z % 8) * 2 + z // 8


def home(group, leaf, half, cell):
    return linear(group * 4 + leaf, half * 8 + cell)


def away(group, leaf, half, cell):
    column = half ^ (leaf // 2)
    z = (4 * QUARTER[leaf] + 3 - cell // 2 + Z_SHIFT) % 16
    return linear(group * 4 + column * 2 + cell % 2, z)


def every_cell():
    for group in range(8):
        for leaf in range(4):
            for half in range(2):
                for cell in range(8):
                    yield group, leaf, half, cell


MOVE_OUT = [(home(*at), away(*at)) for at in every_cell()]
MOVE_BACK = [(there, here) for here, there in MOVE_OUT]
TO_CORE = [(away(g, l, h, c), away(g, l, h, c ^ 1)) for g, l, h, c in every_cell()]
TO_HALF = [(away(g, l, h, c), away(g, l, h ^ 1, c)) for g, l, h, c in every_cell()]
TO_CHIP = [
    (away(g, l, h, c), away(g, l, h, c + (1 if c % 2 else -1)))
    for g, l, h, c in every_cell()
    if 0 <= c + (1 if c % 2 else -1) < 8
]


SAME_CORE = [
    [((group * 4 + column * 2 + core) * 8 + space) * 2 + tm for column in range(2) for space in range(8) for tm in range(2)]
    for group in range(8)
    for core in range(2)
]


def flip(bit):
    return [(i, i ^ bit) for i in range(32)]


def dot(a, b, dims=((1,), (0,)), precision=HIGH):
    return lax.dot_general(a, b, (dims, ((), ())), precision=precision, preferred_element_type=F32)


NT = ((1,), (1,))
TN = ((0,), (0,))


def split(x):
    high = x.astype(jnp.bfloat16)
    return high, (x - high.astype(F32)).astype(jnp.bfloat16)


def dot3(a, b, dims=((1,), (0,))):
    (k,), (m,) = dims
    a_high, a_low = split(a)
    b_high, b_low = split(b)
    plain = functools.partial(
        lax.dot_general, dimension_numbers=(dims, ((), ())), preferred_element_type=F32
    )
    if a.shape[k] < 256:
        first = plain(jnp.concatenate([a_high, a_low], axis=k), jnp.concatenate([b_high, b_high], axis=m))
    else:
        first = plain(a_high, b_high) + plain(a_low, b_high)
    return first + plain(a_high, b_low)


def eliminate(matrix, start, lane, sub):
    stop = start + 16
    inside = (lane >= start) & (lane < stop)
    panel = matrix[start:stop]
    small = [jnp.broadcast_to(panel[:, start + k : start + k + 1], (16, 128)) for k in range(16)]
    rows = jnp.where(inside, (sub == lane - start).astype(F32), panel)
    left = jnp.where(inside, matrix, 0.0)
    for k in range(16):
        scale = 1.0 / small[k][k : k + 1]
        factor = jnp.where(sub == k, -1.0, small[k])

        def step(block):
            return jnp.where(sub == k, 0.0, block) - factor * (block[k : k + 1] * scale)

        for j in range(k + 1, 16):
            small[j] = step(small[j])
        rows = step(rows)
    spread = [jnp.zeros((n, 128), F32) for n in (start, 112 - start) if n]
    spread.insert(1 if start else 0, rows)
    rest = jnp.where(inside, 0.0, matrix) - dot(left, jnp.concatenate(spread, axis=0))
    kept = [rest[stop:]] if stop < 128 else []
    return jnp.concatenate(([rest[:start]] if start else []) + [rows] + kept, axis=0)


def inverses(matrices):
    lane = lax.broadcasted_iota(jnp.int32, (1, 128), 1)
    sub = lax.broadcasted_iota(jnp.int32, (16, 1), 0)

    def step(_, carry):
        out = [eliminate(eliminate(m, 0, lane, sub), 16, lane, sub) for m in carry]
        return tuple(pltpu.roll(jnp.concatenate([m[32:], m[:32]], axis=0), 96, 1) for m in out)

    return lax.fori_loop(0, 4, step, tuple(matrices))


def call(kernel, shapes, *operands, scratch=(), scalars=0):
    smem = pl.BlockSpec(memory_space=pltpu.SMEM)
    vmem = pl.BlockSpec(memory_space=pltpu.VMEM)
    return pl.pallas_call(
        kernel,
        out_shape=[jax.ShapeDtypeStruct(s, F32) for s in shapes],
        in_specs=[smem] * scalars + [vmem] * (len(operands) - scalars),
        out_specs=[vmem] * len(shapes),
        scratch_shapes=list(scratch),
    )(*operands)


def triangles():
    row = lax.broadcasted_iota(jnp.int32, (128, 128), 0)
    column = lax.broadcasted_iota(jnp.int32, (128, 128), 1)
    return row, column


def invert_kernel(blocks, rows, inverse, pack):
    found = inverses([blocks[0:128], blocks[128:256]])
    inverse[0:128] = found[0]
    inverse[128:256] = found[1]
    row, column = triangles()
    pack[0:128] = jnp.where(row >= column, found[0], found[1])
    pack[128:136] = rows[...]
    pack[132:133] = jnp.sum(jnp.where(row == column, found[1], 0.0), axis=0, keepdims=True)


def put_rows(out, first, second):
    out[256:264] = jnp.zeros((8, 512), F32)
    out[256:257, 0:128] = first
    out[256:257, 128:256] = second


def put_half(half, out, blocks, rows):
    early = half == 0
    out[0:128] = jnp.where(early, blocks[1], blocks[0])
    out[128:136] = jnp.zeros((8, 512), F32)
    out[128:129, 0:128] = jnp.where(early, rows[1], rows[0])


def start_kernel(flags, pack, coupling, first, scaled, message, to_half):
    row, column = triangles()
    packed = pack[0:128]
    turned = packed.T
    diagonal = jnp.broadcast_to(pack[132:133], (128, 128))
    inverses_here = [
        jnp.where(row >= column, packed, turned),
        jnp.where(row < column, packed, jnp.where(row > column, turned, diagonal)),
    ]
    blocks, rows = [], []
    for t in range(2):
        at = slice(t * 128, t * 128 + 128)
        weight = pack[130 + t : 131 + t]
        across = jnp.broadcast_to(weight, (128, 128))
        down = across.T
        inverse = inverses_here[t]
        scaled[at] = down * inverse * across
        field = dot3(inverse, coupling[at])
        first[at] = field
        blocks.append(jnp.concatenate([down] * 4, axis=1) * field)
        message[at] = blocks[t]
        rows.append(dot(pack[128 + t : 129 + t], inverse) * weight)
    put_rows(message, *rows)
    put_half(flags[0], to_half, blocks, rows)


def beside(half, own, core, chip, other):
    late = (half == 1).astype(F32)
    weights = (late, 1.0 - late)
    blocks, rows = [], []
    for t in range(2):
        at = slice(t * 128, t * 128 + 128)
        back = slice(128 - t * 128, 256 - t * 128)
        blocks.append(own[back] + core[at] + chip[at] + other[0:128] * weights[t])
        rows.append(
            own[256:257, back] + core[256:257, at] + chip[256:257, at] + other[128:129, 0:128] * weights[t]
        )
    return blocks, rows


def sweep_kernel(flags, scaled, own, core, chip, other, near, message, to_half):
    blocks, rows = beside(flags[0], own, core, chip, other)
    new, new_rows = [], []
    for t in range(2):
        at = slice(t * 128, t * 128 + 128)
        near[at] = blocks[t]
        new.append(dot3(scaled[at], blocks[t]))
        message[at] = new[t]
        new_rows.append(dot(rows[t], scaled[at]))
    put_rows(near, *rows)
    put_rows(message, *new_rows)
    put_half(flags[0], to_half, new, new_rows)


def apply_kernel(flags, scaled, near, message, to_half):
    new, new_rows = [], []
    for t in range(2):
        at = slice(t * 128, t * 128 + 128)
        new.append(dot3(scaled[at], near[at]))
        message[at] = new[t]
        new_rows.append(dot(near[256:257, at], scaled[at]))
    put_rows(message, *new_rows)
    put_half(flags[0], to_half, new, new_rows)


def total_kernel(flags, near0, near1, near2, near3, own, core, chip, other, total):
    blocks, rows = beside(flags[0], own, core, chip, other)
    for t in range(2):
        at = slice(t * 128, t * 128 + 128)
        total[at] = ((near0[at] + near1[at]) + (near2[at] + near3[at])) + blocks[t]
        rows[t] = rows[t] + ((near0[256:257, at] + near1[256:257, at]) + (near2[256:257, at] + near3[256:257, at]))
    put_rows(total, *rows)


def leaf_kernel(inverse, rows, coupling, total, solved, pulled):
    for t in range(2):
        at = slice(t * 128, t * 128 + 128)
        weight = rows[2 + t : 3 + t]
        down = jnp.broadcast_to(weight, (128, 128)).T
        source = coupling[at].astype(F32) + jnp.concatenate([down] * 4, axis=1) * total[at]
        solved[at] = dot3(inverse[at], source)
        row = dot(rows[t : t + 1] + weight * total[256:257, at], inverse[at])
        pulled[0:8, at] = jnp.broadcast_to(row, (8, 128))


def ring_columns(ref, b, count):
    parts = [ref[0:256, ((b + m) % 4) * 128 : ((b + m) % 4) * 128 + 128] for m in range(count)]
    return jnp.concatenate(parts, axis=1)


def gram_early_kernel(pack, coupling, first, own, near, gram, gather):
    for b in range(4):
        count = 3 if b < 2 else 2
        at = slice(b * 128, b * 128 + 128)
        part = dot3(coupling[0:256, at], ring_columns(first, b, count), TN)
        part = part + dot3(own[0:256, at], ring_columns(near, b, count), TN)
        gram[at, 0 : count * 128] = part
        if count == 2:
            gram[at, 256:384] = jnp.zeros((128, 128), F32)
    row = jnp.zeros((1, 512), F32)
    for t in range(2):
        at = slice(t * 128, t * 128 + 128)
        row = row + dot(pack[128 + t : 129 + t], first[at])
        row = row + dot(near[256:257, at], own[at])
    gather[0:8] = jnp.broadcast_to(row, (8, 512))


def gram_late_kernel(
    flags, gram, gather, right, own0, own2, near1, own2_core, chip, other, near2, keep, send, total, both, fields
):
    blocks, rows = beside(flags[0], own2, own2_core, chip, other)
    both[...] = own0[0:256] + own2[0:256]
    row = gather[0:1]
    for t in range(2):
        at = slice(t * 128, t * 128 + 128)
        near2[at] = blocks[t]
        fields[at] = near1[at] + blocks[t]
        row = row + dot(rows[t] + near1[256:257, at], both[at])
    put_rows(near2, *rows)
    for b in range(4):
        count = 3 if b < 2 else 2
        at = slice(b * 128, b * 128 + 128)
        part = gram[at, 0 : count * 128] + dot3(both[0:256, at], ring_columns(fields, b, count), TN)
        for m in range(4):
            for j in range(4):
                source = part[m * 32 + j * 8 : m * 32 + j * 8 + 8]
                total[j % 2, j // 2, b * 32 + m * 8 : b * 32 + m * 8 + 8, 0 : count * 128] = source
                if count == 2:
                    extra = jnp.zeros((8, 128), F32)
                    if b == 2 and m == 0 and j == 0:
                        four = jnp.concatenate([row[:, i * 128 : i * 128 + 128] for i in range(4)], axis=0)
                        extra = jnp.concatenate([four - right[0:4], jnp.zeros((4, 128), F32)], axis=0)
                    total[j % 2, j // 2, b * 32 + m * 8 : b * 32 + m * 8 + 8, 256:384] = extra
    keep[...] = total[flags[1]]
    send[...] = total[1 - flags[1]]


def parent_kernel(
    flags, mine, across_x, across_core, across_both, root_part, upper, solved, solved_row, held
):
    leaf = flags[2]
    held[:, leaf] = mine[...]
    held[:, leaf ^ 2] = across_x[...]
    held[:, leaf ^ 1] = across_core[...]
    held[:, leaf ^ 3] = across_both[...]

    def block(b, m):
        return held[4 * b : 4 * b + 4, :, :, m * 128 : m * 128 + 128].reshape(128, 128)

    entry = {}
    for b in range(4):
        for j in range(b, 4):
            entry[b, j] = block(3, 1).T if (b, j) == (0, 3) else block(b, j - b)
    rhs = [held[4 * b : 4 * b + 4, :, :, 384:640].reshape(128, 256) for b in range(4)]
    reduced = held[8, 0, :, 256:384]
    rows = [reduced[b : b + 1] for b in range(4)]
    part = jnp.zeros((256, 256), F32)
    part_row = jnp.zeros((1, 256), F32)
    upper[...] = jnp.zeros((384, 512), F32)
    for b in range(4):
        (inverse,) = inverses([entry[b, b]])
        wide = jnp.concatenate([entry[b, j] for j in range(b + 1, 4)] + [rhs[b]], axis=1)
        wide = dot(inverse, wide)
        span = (3 - b) * 128
        done = wide[:, span:]
        solved[b * 128 : b * 128 + 128] = done
        row = dot(rows[b], inverse)
        solved_row[0:8, b * 128 : b * 128 + 128] = jnp.broadcast_to(row, (8, 128))
        for i in range(b + 1, 4):
            left = entry[b, i]
            skip = (i - b - 1) * 128
            change = dot(left, wide[:, skip:], TN)
            for j in range(i, 4):
                entry[i, j] = entry[i, j] - change[:, (j - i) * 128 : (j - i) * 128 + 128]
            rhs[i] = rhs[i] - change[:, (4 - i) * 128 :]
            rows[i] = rows[i] - dot(row, left)
            upper[b * 128 : b * 128 + 128, i * 128 : i * 128 + 128] = wide[:, skip : skip + 128]
        part = part + dot(rhs[b], done, TN)
        part_row = part_row + dot(row, rhs[b])
    root_part[0:128] = part[0:128, 0:128]
    root_part[128:256] = part[0:128, 128:256]
    root_part[256:384] = part[128:256, 128:256]
    root_part[384:388] = jnp.broadcast_to(part_row[:, 0:128], (4, 128))
    root_part[388:392] = jnp.broadcast_to(part_row[:, 128:256], (4, 128))


def root_kernel(
    flags, mine, opposite, below, above, matrix, right, upper, solved, solved_row, leaf_solved, pulled, step, parent, move,
):
    part = (mine[...] + opposite[...]) + (below[...] + above[...])
    side = matrix[0:128, 128:256] + part[128:256]
    (first,) = inverses([matrix[0:128, 0:128] + part[0:128]])
    pushed = dot(first, side)
    (second,) = inverses([matrix[128:256, 128:256] + part[256:384] - dot(side, pushed, TN)])
    head = dot(right[0:1, 0:128] - part[384:385], first)
    tail = dot(right[0:1, 128:256] - part[388:389] - dot(head, side), second)
    head = head - dot(tail, pushed, NT)
    root = jnp.concatenate([head, tail], axis=1)
    step[...] = root
    pieces = [None] * 4
    for b in range(3, -1, -1):
        at = slice(b * 128, b * 128 + 128)
        value = solved_row[0:1, at] + dot(root, solved[at], NT)
        for j in range(b + 1, 4):
            value = value - dot(pieces[j], upper[at, j * 128 : j * 128 + 128], NT)
        pieces[b] = value
    chosen = jnp.zeros((1, 128), F32)
    for b in range(4):
        chosen = chosen + jnp.where(flags[3] == b, pieces[b], 0.0)
    chosen = pltpu.roll(jnp.broadcast_to(chosen, (8, 128)), flags[4], 1)
    parent[...] = chosen[0:1, 0:32]
    whole = jnp.concatenate(pieces, axis=1)
    for t in range(2):
        at = slice(t * 128, t * 128 + 128)
        move[t : t + 1] = pulled[0:1, at] - dot(whole, leaf_solved[at], NT)


def neighbours(message, to_half):
    chip = lax.ppermute(message, AXES, TO_CHIP)
    other = lax.ppermute(to_half, AXES, TO_HALF)
    return lax.ppermute(message, AXES, TO_CORE), chip, other


def body(
    coupling, leaf_rhs, conductance, compressor, blocks, parent_of, parent_mat, parent_rhs, link, root_mat, root_rhs
):
    scen = lax.axis_index("scen")
    space = lax.axis_index("space")
    tm = lax.axis_index("tm")
    z = tm * 8 + space
    strip = space * 2 + tm
    quarter = ((z - Z_SHIFT) % 16) // 4
    core = scen % 2
    column = (scen // 2) % 2
    half = column ^ (quarter % 2)
    turn = (128 - (strip % 4) * 32) % 128
    flags = jnp.stack([half, core, scen % 4, strip // 4, turn]).astype(jnp.int32)

    weight = conductance[0] * (1.0 + compressor[0].astype(F32)[..., None]) * 0.5
    own_coupling = coupling[0].reshape(256, 512)
    rows = jnp.concatenate(
        [leaf_rhs[0].reshape(2, 128), weight.reshape(2, 128), jnp.zeros((4, 128), F32)], axis=0
    )
    field = lax.ppermute(own_coupling.astype(F32), AXES, MOVE_OUT)
    own_inverse, own_pack = call(invert_kernel, [(256, 128), (136, 128)], blocks[0].reshape(256, 128), rows)
    pack = lax.ppermute(own_pack, AXES, MOVE_OUT)

    label = parent_of[0]
    sibling = scen % 4
    row_block = strip // 4
    matrix_rows = lax.dynamic_slice(parent_mat, (label, sibling * 8, 0), (1, 8, 512))[0]
    matrix_rows = lax.dynamic_slice(
        jnp.concatenate([matrix_rows, matrix_rows], axis=1), (0, row_block * 128), (8, 384)
    )
    spare = (row_block >= 2) & (lax.broadcasted_iota(jnp.int32, (8, 384), 1) >= 256)
    matrix_rows = jnp.where(spare, 0.0, matrix_rows)
    link_rows = lax.dynamic_slice(link, (label, sibling * 8, 0), (1, 8, 256))[0]
    right = lax.dynamic_slice(parent_rhs, (label, 0), (1, 32))[0] * (sibling == 0).astype(F32)
    right = lax.dynamic_update_slice(jnp.zeros((512,), F32), right, (strip * 32,)).reshape(4, 128)
    right = jnp.concatenate([right, jnp.zeros((4, 128), F32)], axis=0)

    shapes = [(256, 512), (256, 128), (264, 512), (136, 512)]
    first, scaled, own0, half0 = call(start_kernel, shapes, flags, pack, field, scalars=1)
    shapes = [(264, 512), (264, 512), (136, 512)]
    near0, own1, half1 = call(sweep_kernel, shapes, flags, scaled, own0, *neighbours(own0, half0), scalars=1)
    around1 = neighbours(own1, half1)
    gram, gather = call(gram_early_kernel, [(512, 384), (8, 512)], pack, field, first, own0, near0)
    near1, own2, half2 = call(sweep_kernel, shapes, flags, scaled, own1, *around1, scalars=1)
    near2, keep, send = call(
        gram_late_kernel,
        [(264, 512), (2, 128, 384), (2, 128, 384)],
        flags, gram, gather, right, own0, own2, near1, *neighbours(own2, half2),
        scalars=1,
        scratch=[pltpu.VMEM((2, 2, 128, 384), F32), pltpu.VMEM((256, 512), F32), pltpu.VMEM((256, 512), F32)],
    )
    own3, half3 = call(apply_kernel, shapes[1:], flags, scaled, near2, scalars=1)
    around3 = neighbours(own3, half3)
    theirs, _ = lax.optimization_barrier((lax.ppermute(send, "scen", flip(1)), own3))
    half_sum = (keep + theirs).reshape(32, 8, 384)
    shares = lax.all_to_all(half_sum, AXES, 0, 0, axis_index_groups=SAME_CORE)
    near3, own4, half4 = call(sweep_kernel, shapes, flags, scaled, own3, *around3, scalars=1)
    around4 = neighbours(own4, half4)
    shares, _ = lax.optimization_barrier((shares, own4))
    share = jnp.concatenate([jnp.sum(shares, axis=0) + matrix_rows, link_rows], axis=1)
    share = jnp.broadcast_to(share[None], (16, 8, 640))
    mine = lax.all_to_all(share, Z_AXES, 0, 0)
    (total,) = call(total_kernel, [(264, 512)], flags, near0, near1, near2, near3, own4, *around4, scalars=1)
    mine, total = lax.optimization_barrier((mine, total))
    across_x = lax.ppermute(mine, "scen", flip(2))
    across_core = lax.ppermute(mine, "scen", flip(1))
    across_both = lax.ppermute(across_x, "scen", flip(1))

    total = lax.ppermute(total, AXES, MOVE_BACK)
    leaf_solved, pulled = call(leaf_kernel, [(256, 512), (8, 256)], own_inverse, rows, own_coupling, total)

    part, upper, solved, solved_row = call(
        parent_kernel,
        [(392, 128), (384, 512), (512, 256), (8, 512)],
        flags, mine, across_x, across_core, across_both,
        scalars=1,
        scratch=[pltpu.VMEM((16, 4, 8, 640), F32)],
    )
    across, leaf_solved = lax.optimization_barrier((lax.ppermute(part, "scen", flip(4)), leaf_solved))
    part = part + across
    others = [lax.ppermute(part, "scen", [(i, (i + by) % 32) for i in range(32)]) for by in (16, 8, 24)]
    step, parent, move = call(
        root_kernel,
        [(1, 256), (1, 32), (2, 128)],
        flags, part, *others, root_mat, root_rhs.reshape(1, 256), upper, solved, solved_row, leaf_solved, pulled,
        scalars=1,
    )
    return move.reshape(1, 2, 1, 128), parent, step.reshape(256)


def solution(mesh):
    return jax.shard_map(
        body,
        mesh=mesh,
        in_specs=(
            P("scen", "tm", "space", None, None),
            P("scen", "tm", "space", None),
            P("scen", "tm", "space", None),
            P("scen", "tm", "space"),
            P("scen", "tm", "space", None, None),
            P("scen"),
            P(None, ("space", "tm"), None),
            P(None, ("space", "tm")),
            P(None, ("space", "tm"), None),
            P(),
            P(),
        ),
        out_specs=(P("scen", "tm", "space", None), P("scen", ("space", "tm")), P()),
        check_vma=False,
    )
```

```python
import functools

import jax
import jax.numpy as jnp
from jax import lax
from jax.experimental import pallas as pl
from jax.experimental.pallas import tpu as pltpu
from jax.sharding import PartitionSpec as P

AXES = ("scen", "space", "tm")
Z_AXES = ("space", "tm")
F32 = jnp.float32
HIGH = lax.Precision.HIGHEST

QUARTER = (0, 2, 1, 3)
Z_SHIFT = 2


def linear(scen, z):
    return (scen * 8 + z % 8) * 2 + z // 8


def home(group, leaf, half, cell):
    return linear(group * 4 + leaf, half * 8 + cell)


def away(group, leaf, half, cell, side=0):
    column = half ^ (leaf // 2) ^ side
    z = (4 * QUARTER[leaf] + 3 - cell // 2 + Z_SHIFT) % 16
    return linear(group * 4 + column * 2 + cell % 2, z)


def every_cell():
    for group in range(8):
        for leaf in range(4):
            for half in range(2):
                for cell in range(8):
                    yield group, leaf, half, cell


MOVE_OUT = [(home(*at), away(*at)) for at in every_cell()]
MOVE_SIDE = [(home(*at), away(*at, 1)) for at in every_cell()]
MOVE_BACK = [(there, here) for here, there in MOVE_OUT]
TO_CORE = [(away(g, l, h, c), away(g, l, h, c ^ 1)) for g, l, h, c in every_cell()]
TO_HALF = [(away(g, l, h, c), away(g, l, h ^ 1, c)) for g, l, h, c in every_cell()]
TO_CHIP = [
    (away(g, l, h, c), away(g, l, h, c + (1 if c % 2 else -1)))
    for g, l, h, c in every_cell()
    if 0 <= c + (1 if c % 2 else -1) < 8
]


SAME_CORE = [
    [((group * 4 + column * 2 + core) * 8 + space) * 2 + tm for column in range(2) for space in range(8) for tm in range(2)]
    for group in range(8)
    for core in range(2)
]


def flip(bit):
    return [(i, i ^ bit) for i in range(32)]


def dot(a, b, dims=((1,), (0,)), precision=HIGH):
    return lax.dot_general(a, b, (dims, ((), ())), precision=precision, preferred_element_type=F32)


NT = ((1,), (1,))
TN = ((0,), (0,))


def split(x):
    high = x.astype(jnp.bfloat16)
    return high, (x - high.astype(F32)).astype(jnp.bfloat16)


def dot3(a, b, dims=((1,), (0,))):
    (k,), (m,) = dims
    a_high, a_low = split(a)
    b_high, b_low = split(b)
    plain = functools.partial(
        lax.dot_general, dimension_numbers=(dims, ((), ())), preferred_element_type=F32
    )
    if a.shape[k] < 256:
        first = plain(jnp.concatenate([a_high, a_low], axis=k), jnp.concatenate([b_high, b_high], axis=m))
    else:
        first = plain(a_high, b_high) + plain(a_low, b_high)
    return first + plain(a_high, b_low)


def eliminate(matrix, start, lane, sub):
    stop = start + 16
    inside = (lane >= start) & (lane < stop)
    panel = matrix[start:stop]
    small = [jnp.broadcast_to(panel[:, start + k : start + k + 1], (16, 128)) for k in range(16)]
    rows = jnp.where(inside, (sub == lane - start).astype(F32), panel)
    left = jnp.where(inside, matrix, 0.0)
    for k in range(16):
        scale = 1.0 / small[k][k : k + 1]
        factor = jnp.where(sub == k, -1.0, small[k])

        def step(block):
            return jnp.where(sub == k, 0.0, block) - factor * (block[k : k + 1] * scale)

        for j in range(k + 1, 16):
            small[j] = step(small[j])
        rows = step(rows)
    spread = [jnp.zeros((n, 128), F32) for n in (start, 112 - start) if n]
    spread.insert(1 if start else 0, rows)
    rest = jnp.where(inside, 0.0, matrix) - dot(left, jnp.concatenate(spread, axis=0))
    kept = [rest[stop:]] if stop < 128 else []
    return jnp.concatenate(([rest[:start]] if start else []) + [rows] + kept, axis=0)


def inverses(matrices):
    lane = lax.broadcasted_iota(jnp.int32, (1, 128), 1)
    sub = lax.broadcasted_iota(jnp.int32, (16, 1), 0)

    def step(_, carry):
        out = [eliminate(eliminate(m, 0, lane, sub), 16, lane, sub) for m in carry]
        return tuple(pltpu.roll(jnp.concatenate([m[32:], m[:32]], axis=0), 96, 1) for m in out)

    return lax.fori_loop(0, 4, step, tuple(matrices))


def call(kernel, shapes, *operands, scratch=(), scalars=0):
    smem = pl.BlockSpec(memory_space=pltpu.SMEM)
    vmem = pl.BlockSpec(memory_space=pltpu.VMEM)
    return pl.pallas_call(
        kernel,
        out_shape=[jax.ShapeDtypeStruct(s, F32) for s in shapes],
        in_specs=[smem] * scalars + [vmem] * (len(operands) - scalars),
        out_specs=[vmem] * len(shapes),
        scratch_shapes=list(scratch),
    )(*operands)


def triangles():
    row = lax.broadcasted_iota(jnp.int32, (128, 128), 0)
    column = lax.broadcasted_iota(jnp.int32, (128, 128), 1)
    return row, column


def invert_kernel(blocks, rows, inverse, pack):
    found = inverses([blocks[0:128], blocks[128:256]])
    inverse[0:128] = found[0]
    inverse[128:256] = found[1]
    row, column = triangles()
    pack[0:128] = jnp.where(row >= column, found[0], found[1])
    pack[128:136] = rows[...]
    pack[132:133] = jnp.sum(jnp.where(row == column, found[1], 0.0), axis=0, keepdims=True)


def put_rows(out, first, second):
    out[256:264] = jnp.zeros((8, 512), F32)
    out[256:257, 0:128] = first
    out[256:257, 128:256] = second


def put_half(half, out, blocks, rows):
    early = half == 0
    out[0:128] = jnp.where(early, blocks[1], blocks[0])
    out[128:136] = jnp.zeros((8, 512), F32)
    out[128:129, 0:128] = jnp.where(early, rows[1], rows[0])


def start_kernel(flags, pack, early, later, scaled, message, to_half):
    row, column = triangles()
    packed = pack[0:128]
    turned = packed.T
    diagonal = jnp.broadcast_to(pack[132:133], (128, 128))
    inverses_here = [
        jnp.where(row >= column, packed, turned),
        jnp.where(row < column, packed, jnp.where(row > column, turned, diagonal)),
    ]
    blocks, rows = [], []
    for t in range(2):
        at = slice(t * 128, t * 128 + 128)
        weight = pack[130 + t : 131 + t]
        across = jnp.broadcast_to(weight, (128, 128))
        down = across.T
        inverse = inverses_here[t]
        scaled[at] = down * inverse * across
        field = dot3(inverse, (early, later)[t][...])
        blocks.append(jnp.concatenate([down] * 4, axis=1) * field)
        message[at] = blocks[t]
        rows.append(dot(pack[128 + t : 129 + t], inverse) * weight)
    put_rows(message, *rows)
    put_half(flags[0], to_half, blocks, rows)


def beside(half, own, core, chip, other):
    late = (half == 1).astype(F32)
    weights = (late, 1.0 - late)
    blocks, rows = [], []
    for t in range(2):
        at = slice(t * 128, t * 128 + 128)
        back = slice(128 - t * 128, 256 - t * 128)
        blocks.append(own[back] + core[at] + chip[at] + other[0:128] * weights[t])
        rows.append(
            own[256:257, back] + core[256:257, at] + chip[256:257, at] + other[128:129, 0:128] * weights[t]
        )
    return blocks, rows


def sweep_kernel(flags, scaled, own, core, chip, other, near, message, to_half):
    blocks, rows = beside(flags[0], own, core, chip, other)
    new, new_rows = [], []
    for t in range(2):
        at = slice(t * 128, t * 128 + 128)
        near[at] = blocks[t]
        new.append(dot3(scaled[at], blocks[t]))
        message[at] = new[t]
        new_rows.append(dot(rows[t], scaled[at]))
    put_rows(near, *rows)
    put_rows(message, *new_rows)
    put_half(flags[0], to_half, new, new_rows)


def apply_kernel(flags, scaled, near, message, to_half):
    new, new_rows = [], []
    for t in range(2):
        at = slice(t * 128, t * 128 + 128)
        new.append(dot3(scaled[at], near[at]))
        message[at] = new[t]
        new_rows.append(dot(near[256:257, at], scaled[at]))
    put_rows(message, *new_rows)
    put_half(flags[0], to_half, new, new_rows)


def total_kernel(flags, near0, near1, near2, near3, own, core, chip, other, total):
    blocks, rows = beside(flags[0], own, core, chip, other)
    for t in range(2):
        at = slice(t * 128, t * 128 + 128)
        total[at] = ((near0[at] + near1[at]) + (near2[at] + near3[at])) + blocks[t]
        rows[t] = rows[t] + ((near0[256:257, at] + near1[256:257, at]) + (near2[256:257, at] + near3[256:257, at]))
    put_rows(total, *rows)


def leaf_kernel(inverse, rows, coupling, total, solved, pulled):
    for t in range(2):
        at = slice(t * 128, t * 128 + 128)
        weight = rows[2 + t : 3 + t]
        down = jnp.broadcast_to(weight, (128, 128)).T
        source = coupling[at].astype(F32) + jnp.concatenate([down] * 4, axis=1) * total[at]
        solved[at] = dot3(inverse[at], source)
        row = dot(rows[t : t + 1] + weight * total[256:257, at], inverse[at])
        pulled[0:8, at] = jnp.broadcast_to(row, (8, 128))


def ring_columns(ref, b, count):
    parts = [ref[0:256, ((b + m) % 4) * 128 : ((b + m) % 4) * 128 + 128] for m in range(count)]
    return jnp.concatenate(parts, axis=1)


def gram_home_kernel(inverse, rows, coupling, right, gram, gather, first):
    row = -jnp.concatenate([right[i : i + 1] for i in range(4)], axis=1)
    for t in range(2):
        at = slice(t * 128, t * 128 + 128)
        first[at] = dot3(inverse[at], coupling[at].astype(F32))
        row = row + dot(rows[t : t + 1], first[at])
    gather[0:8] = jnp.broadcast_to(row, (8, 512))
    high, low = split(first[...])
    for b in range(4):
        count = 3 if b < 2 else 2
        at = slice(b * 128, b * 128 + 128)
        left = coupling[0:256, at]
        part = None
        for piece in (high, low):
            wide = ring_columns(piece, b, count)
            term = lax.dot_general(left, wide, ((TN), ((), ())), preferred_element_type=F32)
            part = term if part is None else part + term
        gram[at, 0 : count * 128] = part
        if count == 2:
            gram[at, 256:384] = jnp.zeros((128, 128), F32)


def gram_early_kernel(known, known_gather, own, near, gram, gather):
    for b in range(4):
        count = 3 if b < 2 else 2
        at = slice(b * 128, b * 128 + 128)
        part = dot3(own[0:256, at], ring_columns(near, b, count), TN)
        gram[at, 0 : count * 128] = known[at, 0 : count * 128] + part
        if count == 2:
            gram[at, 256:384] = jnp.zeros((128, 128), F32)
    row = known_gather[0:1]
    for t in range(2):
        at = slice(t * 128, t * 128 + 128)
        row = row + dot(near[256:257, at], own[at])
    gather[0:8] = jnp.broadcast_to(row, (8, 512))


def gram_late_kernel(
    flags, gram, gather, own0, own2, near1, own2_core, chip, other, near2, keep, send, total, both, fields
):
    blocks, rows = beside(flags[0], own2, own2_core, chip, other)
    both[...] = own0[0:256] + own2[0:256]
    row = gather[0:1]
    for t in range(2):
        at = slice(t * 128, t * 128 + 128)
        near2[at] = blocks[t]
        fields[at] = near1[at] + blocks[t]
        row = row + dot(rows[t] + near1[256:257, at], both[at])
    put_rows(near2, *rows)
    for b in range(4):
        count = 3 if b < 2 else 2
        at = slice(b * 128, b * 128 + 128)
        part = gram[at, 0 : count * 128] + dot3(both[0:256, at], ring_columns(fields, b, count), TN)
        for m in range(4):
            for j in range(4):
                source = part[m * 32 + j * 8 : m * 32 + j * 8 + 8]
                total[j % 2, j // 2, b * 32 + m * 8 : b * 32 + m * 8 + 8, 0 : count * 128] = source
                if count == 2:
                    extra = jnp.zeros((8, 128), F32)
                    if b == 2 and m == 0 and j == 0:
                        four = jnp.concatenate([row[:, i * 128 : i * 128 + 128] for i in range(4)], axis=0)
                        extra = jnp.concatenate([four, jnp.zeros((4, 128), F32)], axis=0)
                    total[j % 2, j // 2, b * 32 + m * 8 : b * 32 + m * 8 + 8, 256:384] = extra
    keep[...] = total[flags[1]]
    send[...] = total[1 - flags[1]]


def parent_kernel(
    flags, mine, across_x, across_core, across_both, root_part, upper, solved, solved_row, held
):
    leaf = flags[2]
    held[:, leaf] = mine[...]
    held[:, leaf ^ 2] = across_x[...]
    held[:, leaf ^ 1] = across_core[...]
    held[:, leaf ^ 3] = across_both[...]

    def block(b, m):
        return held[4 * b : 4 * b + 4, :, :, m * 128 : m * 128 + 128].reshape(128, 128)

    entry = {}
    for b in range(4):
        for j in range(b, 4):
            entry[b, j] = block(3, 1).T if (b, j) == (0, 3) else block(b, j - b)
    rhs = [held[4 * b : 4 * b + 4, :, :, 384:640].reshape(128, 256) for b in range(4)]
    reduced = held[8, 0, :, 256:384]
    rows = [reduced[b : b + 1] for b in range(4)]
    part = jnp.zeros((256, 256), F32)
    part_row = jnp.zeros((1, 256), F32)
    upper[...] = jnp.zeros((384, 512), F32)
    for b in range(4):
        (inverse,) = inverses([entry[b, b]])
        wide = jnp.concatenate([entry[b, j] for j in range(b + 1, 4)] + [rhs[b]], axis=1)
        wide = dot(inverse, wide)
        span = (3 - b) * 128
        done = wide[:, span:]
        solved[b * 128 : b * 128 + 128] = done
        row = dot(rows[b], inverse)
        solved_row[0:8, b * 128 : b * 128 + 128] = jnp.broadcast_to(row, (8, 128))
        for i in range(b + 1, 4):
            left = entry[b, i]
            skip = (i - b - 1) * 128
            change = dot(left, wide[:, skip:], TN)
            for j in range(i, 4):
                entry[i, j] = entry[i, j] - change[:, (j - i) * 128 : (j - i) * 128 + 128]
            rhs[i] = rhs[i] - change[:, (4 - i) * 128 :]
            rows[i] = rows[i] - dot(row, left)
            upper[b * 128 : b * 128 + 128, i * 128 : i * 128 + 128] = wide[:, skip : skip + 128]
        part = part + dot(rhs[b], done, TN)
        part_row = part_row + dot(row, rhs[b])
    root_part[0:128] = part[0:128, 0:128]
    root_part[128:256] = part[0:128, 128:256]
    root_part[256:384] = part[128:256, 128:256]
    root_part[384:388] = jnp.broadcast_to(part_row[:, 0:128], (4, 128))
    root_part[388:392] = jnp.broadcast_to(part_row[:, 128:256], (4, 128))


def root_kernel(
    flags, mine, opposite, below, above, matrix, right, upper, solved, solved_row, leaf_solved, pulled, step, parent, move,
):
    part = (mine[...] + opposite[...]) + (below[...] + above[...])
    side = matrix[0:128, 128:256] + part[128:256]
    (first,) = inverses([matrix[0:128, 0:128] + part[0:128]])
    pushed = dot(first, side)
    (second,) = inverses([matrix[128:256, 128:256] + part[256:384] - dot(side, pushed, TN)])
    head = dot(right[0:1, 0:128] - part[384:385], first)
    tail = dot(right[0:1, 128:256] - part[388:389] - dot(head, side), second)
    head = head - dot(tail, pushed, NT)
    root = jnp.concatenate([head, tail], axis=1)
    step[...] = root
    pieces = [None] * 4
    for b in range(3, -1, -1):
        at = slice(b * 128, b * 128 + 128)
        value = solved_row[0:1, at] + dot(root, solved[at], NT)
        for j in range(b + 1, 4):
            value = value - dot(pieces[j], upper[at, j * 128 : j * 128 + 128], NT)
        pieces[b] = value
    chosen = jnp.zeros((1, 128), F32)
    for b in range(4):
        chosen = chosen + jnp.where(flags[3] == b, pieces[b], 0.0)
    chosen = pltpu.roll(jnp.broadcast_to(chosen, (8, 128)), flags[4], 1)
    parent[...] = chosen[0:1, 0:32]
    whole = jnp.concatenate(pieces, axis=1)
    for t in range(2):
        at = slice(t * 128, t * 128 + 128)
        move[t : t + 1] = pulled[0:1, at] - dot(whole, leaf_solved[at], NT)


def neighbours(message, to_half):
    chip = lax.ppermute(message, AXES, TO_CHIP)
    other = lax.ppermute(to_half, AXES, TO_HALF)
    return lax.ppermute(message, AXES, TO_CORE), chip, other


def body(
    coupling, leaf_rhs, conductance, compressor, blocks, parent_of, parent_mat, parent_rhs, link, root_mat, root_rhs
):
    scen = lax.axis_index("scen")
    space = lax.axis_index("space")
    tm = lax.axis_index("tm")
    z = tm * 8 + space
    strip = space * 2 + tm
    quarter = ((z - Z_SHIFT) % 16) // 4
    core = scen % 2
    column = (scen // 2) % 2
    half = column ^ (quarter % 2)
    turn = (128 - (strip % 4) * 32) % 128
    flags = jnp.stack([half, core, scen % 4, strip // 4, turn]).astype(jnp.int32)

    weight = conductance[0] * (1.0 + compressor[0].astype(F32)[..., None]) * 0.5
    own_coupling = coupling[0].reshape(256, 512)
    rows = jnp.concatenate(
        [leaf_rhs[0].reshape(2, 128), weight.reshape(2, 128), jnp.zeros((4, 128), F32)], axis=0
    )
    later = lax.ppermute(own_coupling[128:256].astype(F32), AXES, MOVE_SIDE)
    early = lax.ppermute(own_coupling[0:128].astype(F32), AXES, MOVE_OUT)
    own_inverse, own_pack = call(invert_kernel, [(256, 128), (136, 128)], blocks[0].reshape(256, 128), rows)
    pack = lax.ppermute(own_pack, AXES, MOVE_OUT)

    label = parent_of[0]
    sibling = scen % 4
    row_block = strip // 4
    matrix_rows = lax.dynamic_slice(parent_mat, (label, sibling * 8, 0), (1, 8, 512))[0]
    matrix_rows = lax.dynamic_slice(
        jnp.concatenate([matrix_rows, matrix_rows], axis=1), (0, row_block * 128), (8, 384)
    )
    spare = (row_block >= 2) & (lax.broadcasted_iota(jnp.int32, (8, 384), 1) >= 256)
    matrix_rows = jnp.where(spare, 0.0, matrix_rows)
    link_rows = lax.dynamic_slice(link, (label, sibling * 8, 0), (1, 8, 256))[0]
    right = lax.dynamic_slice(parent_rhs, (label, 0), (1, 32))[0] * (sibling == 0).astype(F32)
    right = lax.dynamic_update_slice(jnp.zeros((512,), F32), right, (strip * 32,)).reshape(4, 128)
    right = jnp.concatenate([right, jnp.zeros((4, 128), F32)], axis=0)

    gram, gather = call(
        gram_home_kernel, [(512, 384), (8, 512)], own_inverse, rows, own_coupling, right,
        scratch=[pltpu.VMEM((256, 512), F32)],
    )
    later, gram = lax.optimization_barrier((later, gram))
    later = lax.ppermute(later, "scen", flip(2))
    shapes = [(256, 128), (264, 512), (136, 512)]
    scaled, own0, half0 = call(start_kernel, shapes, flags, pack, early, later, scalars=1)
    shapes = [(264, 512), (264, 512), (136, 512)]
    near0, own1, half1 = call(sweep_kernel, shapes, flags, scaled, own0, *neighbours(own0, half0), scalars=1)
    around1 = neighbours(own1, half1)
    gram, gather = call(gram_early_kernel, [(512, 384), (8, 512)], gram, gather, own0, near0)
    near1, own2, half2 = call(sweep_kernel, shapes, flags, scaled, own1, *around1, scalars=1)
    near2, keep, send = call(
        gram_late_kernel,
        [(264, 512), (2, 128, 384), (2, 128, 384)],
        flags, gram, gather, own0, own2, near1, *neighbours(own2, half2),
        scalars=1,
        scratch=[pltpu.VMEM((2, 2, 128, 384), F32), pltpu.VMEM((256, 512), F32), pltpu.VMEM((256, 512), F32)],
    )
    own3, half3 = call(apply_kernel, shapes[1:], flags, scaled, near2, scalars=1)
    around3 = neighbours(own3, half3)
    theirs, _ = lax.optimization_barrier((lax.ppermute(send, "scen", flip(1)), own3))
    half_sum = (keep + theirs).reshape(32, 8, 384)
    shares = lax.all_to_all(half_sum, AXES, 0, 0, axis_index_groups=SAME_CORE)
    near3, own4, half4 = call(sweep_kernel, shapes, flags, scaled, own3, *around3, scalars=1)
    around4 = neighbours(own4, half4)
    shares, _ = lax.optimization_barrier((shares, own4))
    share = jnp.concatenate([jnp.sum(shares, axis=0) + matrix_rows, link_rows], axis=1)
    share = jnp.broadcast_to(share[None], (16, 8, 640))
    mine = lax.all_to_all(share, Z_AXES, 0, 0)
    (total,) = call(total_kernel, [(264, 512)], flags, near0, near1, near2, near3, own4, *around4, scalars=1)
    mine, total = lax.optimization_barrier((mine, total))
    across_x = lax.ppermute(mine, "scen", flip(2))
    across_core = lax.ppermute(mine, "scen", flip(1))
    across_both = lax.ppermute(across_x, "scen", flip(1))

    total = lax.ppermute(total, AXES, MOVE_BACK)
    leaf_solved, pulled = call(leaf_kernel, [(256, 512), (8, 256)], own_inverse, rows, own_coupling, total)

    part, upper, solved, solved_row = call(
        parent_kernel,
        [(392, 128), (384, 512), (512, 256), (8, 512)],
        flags, mine, across_x, across_core, across_both,
        scalars=1,
        scratch=[pltpu.VMEM((16, 4, 8, 640), F32)],
    )
    across, leaf_solved = lax.optimization_barrier((lax.ppermute(part, "scen", flip(4)), leaf_solved))
    part = part + across
    others = [lax.ppermute(part, "scen", [(i, (i + by) % 32) for i in range(32)]) for by in (16, 8, 24)]
    step, parent, move = call(
        root_kernel,
        [(1, 256), (1, 32), (2, 128)],
        flags, part, *others, root_mat, root_rhs.reshape(1, 256), upper, solved, solved_row, leaf_solved, pulled,
        scalars=1,
    )
    return move.reshape(1, 2, 1, 128), parent, step.reshape(256)


def solution(mesh):
    return jax.shard_map(
        body,
        mesh=mesh,
        in_specs=(
            P("scen", "tm", "space", None, None),
            P("scen", "tm", "space", None),
            P("scen", "tm", "space", None),
            P("scen", "tm", "space"),
            P("scen", "tm", "space", None, None),
            P("scen"),
            P(None, ("space", "tm"), None),
            P(None, ("space", "tm")),
            P(None, ("space", "tm"), None),
            P(),
            P(),
        ),
        out_specs=(P("scen", "tm", "space", None), P("scen", ("space", "tm")), P()),
        check_vma=False,
    )
```

```python
import functools

import jax
import jax.numpy as jnp
from jax import lax
from jax.experimental import pallas as pl
from jax.experimental.pallas import tpu as pltpu
from jax.sharding import PartitionSpec as P

AXES = ("scen", "space", "tm")
Z_AXES = ("space", "tm")
F32 = jnp.float32
HIGH = lax.Precision.HIGHEST

QUARTER = (0, 2, 1, 3)
Z_SHIFT = 2


def linear(scen, z):
    return (scen * 8 + z % 8) * 2 + z // 8


def home(group, leaf, half, cell):
    return linear(group * 4 + leaf, half * 8 + cell)


def away(group, leaf, half, cell):
    column = half ^ (leaf // 2)
    z = (4 * QUARTER[leaf] + 3 - cell // 2 + Z_SHIFT) % 16
    return linear(group * 4 + column * 2 + cell % 2, z)


def every_cell():
    for group in range(8):
        for leaf in range(4):
            for half in range(2):
                for cell in range(8):
                    yield group, leaf, half, cell


MOVE_OUT = [(home(*at), away(*at)) for at in every_cell()]
MOVE_BACK = [(there, here) for here, there in MOVE_OUT]
TO_CORE = [(away(g, l, h, c), away(g, l, h, c ^ 1)) for g, l, h, c in every_cell()]
TO_HALF = [(away(g, l, h, c), away(g, l, h ^ 1, c)) for g, l, h, c in every_cell()]
TO_CHIP = [
    (away(g, l, h, c), away(g, l, h, c + (1 if c % 2 else -1)))
    for g, l, h, c in every_cell()
    if 0 <= c + (1 if c % 2 else -1) < 8
]


SAME_CORE = [
    [((group * 4 + column * 2 + core) * 8 + space) * 2 + tm for column in range(2) for space in range(8) for tm in range(2)]
    for group in range(8)
    for core in range(2)
]


def flip(bit):
    return [(i, i ^ bit) for i in range(32)]


def dot(a, b, dims=((1,), (0,)), precision=HIGH):
    return lax.dot_general(a, b, (dims, ((), ())), precision=precision, preferred_element_type=F32)


NT = ((1,), (1,))
TN = ((0,), (0,))


def split(x):
    high = x.astype(jnp.bfloat16)
    return high, (x - high.astype(F32)).astype(jnp.bfloat16)


def dot3(a, b, dims=((1,), (0,))):
    (k,), (m,) = dims
    a_high, a_low = split(a)
    b_high, b_low = split(b)
    plain = functools.partial(
        lax.dot_general, dimension_numbers=(dims, ((), ())), preferred_element_type=F32
    )
    if a.shape[k] < 256:
        first = plain(jnp.concatenate([a_high, a_low], axis=k), jnp.concatenate([b_high, b_high], axis=m))
    else:
        first = plain(a_high, b_high) + plain(a_low, b_high)
    return first + plain(a_high, b_low)


def eliminate(matrix, start, lane, sub):
    stop = start + 16
    inside = (lane >= start) & (lane < stop)
    panel = matrix[start:stop]
    small = [jnp.broadcast_to(panel[:, start + k : start + k + 1], (16, 128)) for k in range(16)]
    rows = jnp.where(inside, (sub == lane - start).astype(F32), panel)
    left = jnp.where(inside, matrix, 0.0)
    for k in range(16):
        scale = 1.0 / small[k][k : k + 1]
        factor = jnp.where(sub == k, -1.0, small[k])

        def step(block):
            return jnp.where(sub == k, 0.0, block) - factor * (block[k : k + 1] * scale)

        for j in range(k + 1, 16):
            small[j] = step(small[j])
        rows = step(rows)
    spread = [jnp.zeros((n, 128), F32) for n in (start, 112 - start) if n]
    spread.insert(1 if start else 0, rows)
    rest = jnp.where(inside, 0.0, matrix) - dot(left, jnp.concatenate(spread, axis=0))
    kept = [rest[stop:]] if stop < 128 else []
    return jnp.concatenate(([rest[:start]] if start else []) + [rows] + kept, axis=0)


def inverses(matrices):
    lane = lax.broadcasted_iota(jnp.int32, (1, 128), 1)
    sub = lax.broadcasted_iota(jnp.int32, (16, 1), 0)

    def step(_, carry):
        out = [eliminate(eliminate(m, 0, lane, sub), 16, lane, sub) for m in carry]
        return tuple(pltpu.roll(jnp.concatenate([m[32:], m[:32]], axis=0), 96, 1) for m in out)

    return lax.fori_loop(0, 4, step, tuple(matrices))


def call(kernel, shapes, *operands, scratch=(), scalars=0):
    smem = pl.BlockSpec(memory_space=pltpu.SMEM)
    vmem = pl.BlockSpec(memory_space=pltpu.VMEM)
    return pl.pallas_call(
        kernel,
        out_shape=[jax.ShapeDtypeStruct(s, F32) for s in shapes],
        in_specs=[smem] * scalars + [vmem] * (len(operands) - scalars),
        out_specs=[vmem] * len(shapes),
        scratch_shapes=list(scratch),
    )(*operands)


def triangles():
    row = lax.broadcasted_iota(jnp.int32, (128, 128), 0)
    column = lax.broadcasted_iota(jnp.int32, (128, 128), 1)
    return row, column


def invert_kernel(blocks, rows, inverse, pack):
    found = inverses([blocks[0:128], blocks[128:256]])
    inverse[0:128] = found[0]
    inverse[128:256] = found[1]
    row, column = triangles()
    pack[0:128] = jnp.where(row >= column, found[0], found[1])
    pack[128:136] = rows[...]
    pack[132:133] = jnp.sum(jnp.where(row == column, found[1], 0.0), axis=0, keepdims=True)


def put_rows(out, first, second):
    out[256:264] = jnp.zeros((8, 512), F32)
    out[256:257, 0:128] = first
    out[256:257, 128:256] = second


def put_half(half, out, blocks, rows):
    early = half == 0
    out[0:128] = jnp.where(early, blocks[1], blocks[0])
    out[128:136] = jnp.zeros((8, 512), F32)
    out[128:129, 0:128] = jnp.where(early, rows[1], rows[0])


def start_kernel(flags, pack, coupling, scaled, message, to_half):
    row, column = triangles()
    packed = pack[0:128]
    turned = packed.T
    diagonal = jnp.broadcast_to(pack[132:133], (128, 128))
    inverses_here = [
        jnp.where(row >= column, packed, turned),
        jnp.where(row < column, packed, jnp.where(row > column, turned, diagonal)),
    ]
    blocks, rows = [], []
    for t in range(2):
        at = slice(t * 128, t * 128 + 128)
        weight = pack[130 + t : 131 + t]
        across = jnp.broadcast_to(weight, (128, 128))
        down = across.T
        inverse = inverses_here[t]
        scaled[at] = down * inverse * across
        field = dot3(inverse, coupling[at])
        blocks.append(jnp.concatenate([down] * 4, axis=1) * field)
        message[at] = blocks[t]
        rows.append(dot(pack[128 + t : 129 + t], inverse) * weight)
    put_rows(message, *rows)
    put_half(flags[0], to_half, blocks, rows)


def beside(half, own, core, chip, other):
    late = (half == 1).astype(F32)
    weights = (late, 1.0 - late)
    blocks, rows = [], []
    for t in range(2):
        at = slice(t * 128, t * 128 + 128)
        back = slice(128 - t * 128, 256 - t * 128)
        blocks.append(own[back] + core[at] + chip[at] + other[0:128] * weights[t])
        rows.append(
            own[256:257, back] + core[256:257, at] + chip[256:257, at] + other[128:129, 0:128] * weights[t]
        )
    return blocks, rows


def sweep_kernel(flags, scaled, own, core, chip, other, near, message, to_half):
    blocks, rows = beside(flags[0], own, core, chip, other)
    new, new_rows = [], []
    for t in range(2):
        at = slice(t * 128, t * 128 + 128)
        near[at] = blocks[t]
        new.append(dot3(scaled[at], blocks[t]))
        message[at] = new[t]
        new_rows.append(dot(rows[t], scaled[at]))
    put_rows(near, *rows)
    put_rows(message, *new_rows)
    put_half(flags[0], to_half, new, new_rows)


def apply_kernel(flags, scaled, near, message, to_half):
    new, new_rows = [], []
    for t in range(2):
        at = slice(t * 128, t * 128 + 128)
        new.append(dot3(scaled[at], near[at]))
        message[at] = new[t]
        new_rows.append(dot(near[256:257, at], scaled[at]))
    put_rows(message, *new_rows)
    put_half(flags[0], to_half, new, new_rows)


def total_kernel(flags, near0, near1, near2, near3, own, core, chip, other, total):
    blocks, rows = beside(flags[0], own, core, chip, other)
    for t in range(2):
        at = slice(t * 128, t * 128 + 128)
        total[at] = ((near0[at] + near1[at]) + (near2[at] + near3[at])) + blocks[t]
        rows[t] = rows[t] + ((near0[256:257, at] + near1[256:257, at]) + (near2[256:257, at] + near3[256:257, at]))
    put_rows(total, *rows)


def leaf_kernel(inverse, rows, coupling, total, solved, pulled):
    for t in range(2):
        at = slice(t * 128, t * 128 + 128)
        weight = rows[2 + t : 3 + t]
        down = jnp.broadcast_to(weight, (128, 128)).T
        source = coupling[at].astype(F32) + jnp.concatenate([down] * 4, axis=1) * total[at]
        solved[at] = dot3(inverse[at], source)
        row = dot(rows[t : t + 1] + weight * total[256:257, at], inverse[at])
        pulled[0:8, at] = jnp.broadcast_to(row, (8, 128))


def ring_columns(ref, b, count):
    parts = [ref[0:256, ((b + m) % 4) * 128 : ((b + m) % 4) * 128 + 128] for m in range(count)]
    return jnp.concatenate(parts, axis=1)


def gram_home_kernel(inverse, rows, coupling, right, gram, gather, first):
    row = -jnp.concatenate([right[i : i + 1] for i in range(4)], axis=1)
    for t in range(2):
        at = slice(t * 128, t * 128 + 128)
        first[at] = dot3(inverse[at], coupling[at].astype(F32))
        row = row + dot(rows[t : t + 1], first[at])
    gather[0:8] = jnp.broadcast_to(row, (8, 512))
    high, low = split(first[...])
    for b in range(4):
        count = 3 if b < 2 else 2
        at = slice(b * 128, b * 128 + 128)
        left = coupling[0:256, at]
        part = None
        for piece in (high, low):
            wide = ring_columns(piece, b, count)
            term = lax.dot_general(left, wide, ((TN), ((), ())), preferred_element_type=F32)
            part = term if part is None else part + term
        gram[at, 0 : count * 128] = part
        if count == 2:
            gram[at, 256:384] = jnp.zeros((128, 128), F32)


def gram_early_kernel(known, known_gather, own, near, gram, gather):
    for b in range(4):
        count = 3 if b < 2 else 2
        at = slice(b * 128, b * 128 + 128)
        part = dot3(own[0:256, at], ring_columns(near, b, count), TN)
        gram[at, 0 : count * 128] = known[at, 0 : count * 128] + part
        if count == 2:
            gram[at, 256:384] = jnp.zeros((128, 128), F32)
    row = known_gather[0:1]
    for t in range(2):
        at = slice(t * 128, t * 128 + 128)
        row = row + dot(near[256:257, at], own[at])
    gather[0:8] = jnp.broadcast_to(row, (8, 512))


def gram_late_kernel(
    flags, gram, gather, own0, own2, near1, own2_core, chip, other, near2, keep, send, total, both, fields
):
    blocks, rows = beside(flags[0], own2, own2_core, chip, other)
    both[...] = own0[0:256] + own2[0:256]
    row = gather[0:1]
    for t in range(2):
        at = slice(t * 128, t * 128 + 128)
        near2[at] = blocks[t]
        fields[at] = near1[at] + blocks[t]
        row = row + dot(rows[t] + near1[256:257, at], both[at])
    put_rows(near2, *rows)
    for b in range(4):
        count = 3 if b < 2 else 2
        at = slice(b * 128, b * 128 + 128)
        part = gram[at, 0 : count * 128] + dot3(both[0:256, at], ring_columns(fields, b, count), TN)
        for m in range(4):
            for j in range(4):
                source = part[m * 32 + j * 8 : m * 32 + j * 8 + 8]
                total[j % 2, j // 2, b * 32 + m * 8 : b * 32 + m * 8 + 8, 0 : count * 128] = source
                if count == 2:
                    extra = jnp.zeros((8, 128), F32)
                    if b == 2 and m == 0 and j == 0:
                        four = jnp.concatenate([row[:, i * 128 : i * 128 + 128] for i in range(4)], axis=0)
                        extra = jnp.concatenate([four, jnp.zeros((4, 128), F32)], axis=0)
                    total[j % 2, j // 2, b * 32 + m * 8 : b * 32 + m * 8 + 8, 256:384] = extra
    keep[...] = total[flags[1]]
    send[...] = total[1 - flags[1]]


def parent_kernel(
    flags, mine, across_x, across_core, across_both, root_part, upper, solved, solved_row, held
):
    leaf = flags[2]
    held[:, leaf] = mine[...]
    held[:, leaf ^ 2] = across_x[...]
    held[:, leaf ^ 1] = across_core[...]
    held[:, leaf ^ 3] = across_both[...]

    def block(b, m):
        return held[4 * b : 4 * b + 4, :, :, m * 128 : m * 128 + 128].reshape(128, 128)

    entry = {}
    for b in range(4):
        for j in range(b, 4):
            entry[b, j] = block(3, 1).T if (b, j) == (0, 3) else block(b, j - b)
    rhs = [held[4 * b : 4 * b + 4, :, :, 384:640].reshape(128, 256) for b in range(4)]
    reduced = held[8, 0, :, 256:384]
    rows = [reduced[b : b + 1] for b in range(4)]
    part = jnp.zeros((256, 256), F32)
    part_row = jnp.zeros((1, 256), F32)
    upper[...] = jnp.zeros((384, 512), F32)
    for b in range(4):
        (inverse,) = inverses([entry[b, b]])
        wide = jnp.concatenate([entry[b, j] for j in range(b + 1, 4)] + [rhs[b]], axis=1)
        wide = dot(inverse, wide)
        span = (3 - b) * 128
        done = wide[:, span:]
        solved[b * 128 : b * 128 + 128] = done
        row = dot(rows[b], inverse)
        solved_row[0:8, b * 128 : b * 128 + 128] = jnp.broadcast_to(row, (8, 128))
        for i in range(b + 1, 4):
            left = entry[b, i]
            skip = (i - b - 1) * 128
            change = dot(left, wide[:, skip:], TN)
            for j in range(i, 4):
                entry[i, j] = entry[i, j] - change[:, (j - i) * 128 : (j - i) * 128 + 128]
            rhs[i] = rhs[i] - change[:, (4 - i) * 128 :]
            rows[i] = rows[i] - dot(row, left)
            upper[b * 128 : b * 128 + 128, i * 128 : i * 128 + 128] = wide[:, skip : skip + 128]
        part = part + dot3(rhs[b], done, TN)
        part_row = part_row + dot(row, rhs[b])
    root_part[0:128] = part[0:128, 0:128]
    root_part[128:256] = part[0:128, 128:256]
    root_part[256:384] = part[128:256, 128:256]
    root_part[384:388] = jnp.broadcast_to(part_row[:, 0:128], (4, 128))
    root_part[388:392] = jnp.broadcast_to(part_row[:, 128:256], (4, 128))


def back_kernel(upper, solved, solved_row, leaf_solved, pulled, link_solved, vector, reach, base):
    pieces, rows = [None] * 4, [None] * 4
    for b in range(3, -1, -1):
        at = slice(b * 128, b * 128 + 128)
        piece, row = solved[at], solved_row[0:1, at]
        if b < 3:
            after = upper[at, b * 128 + 128 : 512]
            piece = piece - dot(after, jnp.concatenate(pieces[b + 1 :], axis=0))
            row = row - dot(jnp.concatenate(rows[b + 1 :], axis=1), after, NT)
        pieces[b], rows[b] = piece, row
        link_solved[at] = piece
    whole = jnp.concatenate(rows, axis=1)
    vector[...] = jnp.broadcast_to(whole, (8, 512))
    reach[...] = dot(leaf_solved[...], jnp.concatenate(pieces, axis=0))
    base[...] = jnp.broadcast_to(pulled[0:1] - dot(whole, leaf_solved[...], NT), (8, 256))


def root_kernel(
    flags, mine, opposite, below, above, matrix, right, link_solved, vector, reach, base, step, parent, move
):
    part = (mine[...] + opposite[...]) + (below[...] + above[...])
    side = matrix[0:128, 128:256] + part[128:256]
    (first,) = inverses([matrix[0:128, 0:128] + part[0:128]])
    pushed = dot(first, side)
    (second,) = inverses([matrix[128:256, 128:256] + part[256:384] - dot(side, pushed, TN)])
    head = dot(right[0:1, 0:128] - part[384:385], first)
    tail = dot(right[0:1, 128:256] - part[388:389] - dot(head, side), second)
    head = head - dot(tail, pushed, NT)
    root = jnp.concatenate([head, tail], axis=1)
    step[...] = root
    whole = vector[0:1] + dot(root, link_solved[...], NT)
    last = base[0:1] - dot(root, reach[...], NT)
    for t in range(2):
        move[t : t + 1] = last[:, t * 128 : t * 128 + 128]
    chosen = jnp.zeros((1, 128), F32)
    for b in range(4):
        chosen = chosen + jnp.where(flags[3] == b, whole[:, b * 128 : b * 128 + 128], 0.0)
    chosen = pltpu.roll(jnp.broadcast_to(chosen, (8, 128)), flags[4], 1)
    parent[...] = chosen[0:1, 0:32]


def neighbours(message, to_half):
    chip = lax.ppermute(message, AXES, TO_CHIP)
    other = lax.ppermute(to_half, AXES, TO_HALF)
    return lax.ppermute(message, AXES, TO_CORE), chip, other


def body(
    coupling, leaf_rhs, conductance, compressor, blocks, parent_of, parent_mat, parent_rhs, link, root_mat, root_rhs
):
    scen = lax.axis_index("scen")
    space = lax.axis_index("space")
    tm = lax.axis_index("tm")
    z = tm * 8 + space
    strip = space * 2 + tm
    quarter = ((z - Z_SHIFT) % 16) // 4
    core = scen % 2
    column = (scen // 2) % 2
    half = column ^ (quarter % 2)
    turn = (128 - (strip % 4) * 32) % 128
    flags = jnp.stack([half, core, scen % 4, strip // 4, turn]).astype(jnp.int32)

    weight = conductance[0] * (1.0 + compressor[0].astype(F32)[..., None]) * 0.5
    own_coupling = coupling[0].reshape(256, 512)
    rows = jnp.concatenate(
        [leaf_rhs[0].reshape(2, 128), weight.reshape(2, 128), jnp.zeros((4, 128), F32)], axis=0
    )
    field = lax.ppermute(own_coupling.astype(F32), AXES, MOVE_OUT)
    own_inverse, own_pack = call(invert_kernel, [(256, 128), (136, 128)], blocks[0].reshape(256, 128), rows)
    pack = lax.ppermute(own_pack, AXES, MOVE_OUT)

    label = parent_of[0]
    sibling = scen % 4
    row_block = strip // 4
    matrix_rows = lax.dynamic_slice(parent_mat, (label, sibling * 8, 0), (1, 8, 512))[0]
    matrix_rows = lax.dynamic_slice(
        jnp.concatenate([matrix_rows, matrix_rows], axis=1), (0, row_block * 128), (8, 384)
    )
    spare = (row_block >= 2) & (lax.broadcasted_iota(jnp.int32, (8, 384), 1) >= 256)
    matrix_rows = jnp.where(spare, 0.0, matrix_rows)
    link_rows = lax.dynamic_slice(link, (label, sibling * 8, 0), (1, 8, 256))[0]
    right = lax.dynamic_slice(parent_rhs, (label, 0), (1, 32))[0] * (sibling == 0).astype(F32)
    right = lax.dynamic_update_slice(jnp.zeros((512,), F32), right, (strip * 32,)).reshape(4, 128)
    right = jnp.concatenate([right, jnp.zeros((4, 128), F32)], axis=0)

    gram, gather = call(
        gram_home_kernel, [(512, 384), (8, 512)], own_inverse, rows, own_coupling, right,
        scratch=[pltpu.VMEM((256, 512), F32)],
    )
    pack, gram = lax.optimization_barrier((pack, gram))
    shapes = [(256, 128), (264, 512), (136, 512)]
    scaled, own0, half0 = call(start_kernel, shapes, flags, pack, field, scalars=1)
    shapes = [(264, 512), (264, 512), (136, 512)]
    near0, own1, half1 = call(sweep_kernel, shapes, flags, scaled, own0, *neighbours(own0, half0), scalars=1)
    around1 = neighbours(own1, half1)
    gram, gather = call(gram_early_kernel, [(512, 384), (8, 512)], gram, gather, own0, near0)
    near1, own2, half2 = call(sweep_kernel, shapes, flags, scaled, own1, *around1, scalars=1)
    near2, keep, send = call(
        gram_late_kernel,
        [(264, 512), (2, 128, 384), (2, 128, 384)],
        flags, gram, gather, own0, own2, near1, *neighbours(own2, half2),
        scalars=1,
        scratch=[pltpu.VMEM((2, 2, 128, 384), F32), pltpu.VMEM((256, 512), F32), pltpu.VMEM((256, 512), F32)],
    )
    own3, half3 = call(apply_kernel, shapes[1:], flags, scaled, near2, scalars=1)
    around3 = neighbours(own3, half3)
    theirs, _ = lax.optimization_barrier((lax.ppermute(send, "scen", flip(1)), own3))
    half_sum = (keep + theirs).reshape(32, 8, 384)
    shares = lax.all_to_all(half_sum, AXES, 0, 0, axis_index_groups=SAME_CORE)
    near3, own4, half4 = call(sweep_kernel, shapes, flags, scaled, own3, *around3, scalars=1)
    around4 = neighbours(own4, half4)
    shares, _ = lax.optimization_barrier((shares, own4))
    share = jnp.concatenate([jnp.sum(shares, axis=0) + matrix_rows, link_rows], axis=1)
    share = jnp.broadcast_to(share[None], (16, 8, 640))
    mine = lax.all_to_all(share, Z_AXES, 0, 0)
    (total,) = call(total_kernel, [(264, 512)], flags, near0, near1, near2, near3, own4, *around4, scalars=1)
    mine, total = lax.optimization_barrier((mine, total))
    across_x = lax.ppermute(mine, "scen", flip(2))
    across_core = lax.ppermute(mine, "scen", flip(1))
    across_both = lax.ppermute(across_x, "scen", flip(1))

    total = lax.ppermute(total, AXES, MOVE_BACK)
    leaf_solved, pulled = call(leaf_kernel, [(256, 512), (8, 256)], own_inverse, rows, own_coupling, total)

    part, upper, solved, solved_row = call(
        parent_kernel,
        [(392, 128), (384, 512), (512, 256), (8, 512)],
        flags, mine, across_x, across_core, across_both,
        scalars=1,
        scratch=[pltpu.VMEM((16, 4, 8, 640), F32)],
    )
    across, leaf_solved = lax.optimization_barrier((lax.ppermute(part, "scen", flip(4)), leaf_solved))
    part = part + across
    others = [lax.ppermute(part, "scen", [(i, (i + by) % 32) for i in range(32)]) for by in (16, 8, 24)]
    link_solved, vector, reach, base = call(
        back_kernel, [(512, 256), (8, 512), (256, 256), (8, 256)], upper, solved, solved_row, leaf_solved, pulled
    )
    others[2], link_solved = lax.optimization_barrier((others[2], link_solved))
    step, parent, move = call(
        root_kernel,
        [(1, 256), (1, 32), (2, 128)],
        flags, part, *others, root_mat, root_rhs.reshape(1, 256), link_solved, vector, reach, base,
        scalars=1,
    )
    return move.reshape(1, 2, 1, 128), parent, step.reshape(256)


def solution(mesh):
    return jax.shard_map(
        body,
        mesh=mesh,
        in_specs=(
            P("scen", "tm", "space", None, None),
            P("scen", "tm", "space", None),
            P("scen", "tm", "space", None),
            P("scen", "tm", "space"),
            P("scen", "tm", "space", None, None),
            P("scen"),
            P(None, ("space", "tm"), None),
            P(None, ("space", "tm")),
            P(None, ("space", "tm"), None),
            P(),
            P(),
        ),
        out_specs=(P("scen", "tm", "space", None), P("scen", ("space", "tm")), P()),
        check_vma=False,
    )
```

```python
import functools

import jax
import jax.numpy as jnp
from jax import lax
from jax.experimental import pallas as pl
from jax.experimental.pallas import tpu as pltpu
from jax.sharding import PartitionSpec as P

AXES = ("scen", "space", "tm")
Z_AXES = ("space", "tm")
F32 = jnp.float32
HIGH = lax.Precision.HIGHEST

QUARTER = (0, 2, 1, 3)
Z_SHIFT = 2


def linear(scen, z):
    return (scen * 8 + z % 8) * 2 + z // 8


def home(group, leaf, half, cell):
    return linear(group * 4 + leaf, half * 8 + cell)


def away(group, leaf, half, cell):
    column = half ^ (leaf // 2)
    z = (4 * QUARTER[leaf] + 3 - cell // 2 + Z_SHIFT) % 16
    return linear(group * 4 + column * 2 + cell % 2, z)


def every_cell():
    for group in range(8):
        for leaf in range(4):
            for half in range(2):
                for cell in range(8):
                    yield group, leaf, half, cell


MOVE_OUT = [(home(*at), away(*at)) for at in every_cell()]
MOVE_BACK = [(there, here) for here, there in MOVE_OUT]
TO_CORE = [(away(g, l, h, c), away(g, l, h, c ^ 1)) for g, l, h, c in every_cell()]
TO_HALF = [(away(g, l, h, c), away(g, l, h ^ 1, c)) for g, l, h, c in every_cell()]
TO_CHIP = [
    (away(g, l, h, c), away(g, l, h, c + (1 if c % 2 else -1)))
    for g, l, h, c in every_cell()
    if 0 <= c + (1 if c % 2 else -1) < 8
]


SAME_CORE = [
    [((group * 4 + column * 2 + core) * 8 + space) * 2 + tm for column in range(2) for space in range(8) for tm in range(2)]
    for group in range(8)
    for core in range(2)
]


def flip(bit):
    return [(i, i ^ bit) for i in range(32)]


def dot(a, b, dims=((1,), (0,)), precision=HIGH):
    return lax.dot_general(a, b, (dims, ((), ())), precision=precision, preferred_element_type=F32)


NT = ((1,), (1,))
TN = ((0,), (0,))


def split(x):
    high = x.astype(jnp.bfloat16)
    return high, (x - high.astype(F32)).astype(jnp.bfloat16)


def dot3(a, b, dims=((1,), (0,))):
    (k,), (m,) = dims
    a_high, a_low = split(a)
    b_high, b_low = split(b)
    plain = functools.partial(
        lax.dot_general, dimension_numbers=(dims, ((), ())), preferred_element_type=F32
    )
    if a.shape[k] < 256:
        first = plain(jnp.concatenate([a_high, a_low], axis=k), jnp.concatenate([b_high, b_high], axis=m))
    else:
        first = plain(a_high, b_high) + plain(a_low, b_high)
    return first + plain(a_high, b_low)


def eliminate(matrix, start, lane, sub):
    stop = start + 16
    inside = (lane >= start) & (lane < stop)
    panel = matrix[start:stop]
    small = [jnp.broadcast_to(panel[:, start + k : start + k + 1], (16, 128)) for k in range(16)]
    rows = jnp.where(inside, (sub == lane - start).astype(F32), panel)
    left = jnp.where(inside, matrix, 0.0)
    for k in range(16):
        scale = 1.0 / small[k][k : k + 1]
        factor = jnp.where(sub == k, -1.0, small[k])

        def step(block):
            return jnp.where(sub == k, 0.0, block) - factor * (block[k : k + 1] * scale)

        for j in range(k + 1, 16):
            small[j] = step(small[j])
        rows = step(rows)
    spread = [jnp.zeros((n, 128), F32) for n in (start, 112 - start) if n]
    spread.insert(1 if start else 0, rows)
    rest = jnp.where(inside, 0.0, matrix) - dot(left, jnp.concatenate(spread, axis=0))
    kept = [rest[stop:]] if stop < 128 else []
    return jnp.concatenate(([rest[:start]] if start else []) + [rows] + kept, axis=0)


def inverses(matrices):
    lane = lax.broadcasted_iota(jnp.int32, (1, 128), 1)
    sub = lax.broadcasted_iota(jnp.int32, (16, 1), 0)

    def step(_, carry):
        out = [eliminate(eliminate(m, 0, lane, sub), 16, lane, sub) for m in carry]
        return tuple(pltpu.roll(jnp.concatenate([m[32:], m[:32]], axis=0), 96, 1) for m in out)

    return lax.fori_loop(0, 4, step, tuple(matrices))


def call(kernel, shapes, *operands, scratch=(), scalars=0):
    smem = pl.BlockSpec(memory_space=pltpu.SMEM)
    vmem = pl.BlockSpec(memory_space=pltpu.VMEM)
    return pl.pallas_call(
        kernel,
        out_shape=[jax.ShapeDtypeStruct(s, F32) for s in shapes],
        in_specs=[smem] * scalars + [vmem] * (len(operands) - scalars),
        out_specs=[vmem] * len(shapes),
        scratch_shapes=list(scratch),
    )(*operands)


def triangles():
    row = lax.broadcasted_iota(jnp.int32, (128, 128), 0)
    column = lax.broadcasted_iota(jnp.int32, (128, 128), 1)
    return row, column


def invert_kernel(blocks, rows, inverse, pack):
    found = inverses([blocks[0:128], blocks[128:256]])
    inverse[0:128] = found[0]
    inverse[128:256] = found[1]
    row, column = triangles()
    pack[0:128] = jnp.where(row >= column, found[0], found[1])
    pack[128:136] = rows[...]
    pack[132:133] = jnp.sum(jnp.where(row == column, found[1], 0.0), axis=0, keepdims=True)


def put_rows(out, first, second):
    out[256:264] = jnp.zeros((8, 512), F32)
    out[256:257, 0:128] = first
    out[256:257, 128:256] = second


def put_half(half, out, blocks, rows):
    early = half == 0
    out[0:128] = jnp.where(early, blocks[1], blocks[0])
    out[128:136] = jnp.zeros((8, 512), F32)
    out[128:129, 0:128] = jnp.where(early, rows[1], rows[0])


def start_kernel(flags, pack, coupling, scaled, message, to_half):
    row, column = triangles()
    packed = pack[0:128]
    turned = packed.T
    diagonal = jnp.broadcast_to(pack[132:133], (128, 128))
    inverses_here = [
        jnp.where(row >= column, packed, turned),
        jnp.where(row < column, packed, jnp.where(row > column, turned, diagonal)),
    ]
    blocks, rows = [], []
    for t in range(2):
        at = slice(t * 128, t * 128 + 128)
        weight = pack[130 + t : 131 + t]
        across = jnp.broadcast_to(weight, (128, 128))
        down = across.T
        inverse = inverses_here[t]
        scaled[at] = down * inverse * across
        field = dot3(inverse, coupling[at])
        blocks.append(jnp.concatenate([down] * 4, axis=1) * field)
        message[at] = blocks[t]
        rows.append(dot(pack[128 + t : 129 + t], inverse) * weight)
    put_rows(message, *rows)
    put_half(flags[0], to_half, blocks, rows)


def beside(half, own, core, chip, other):
    late = (half == 1).astype(F32)
    weights = (late, 1.0 - late)
    blocks, rows = [], []
    for t in range(2):
        at = slice(t * 128, t * 128 + 128)
        back = slice(128 - t * 128, 256 - t * 128)
        blocks.append(own[back] + core[at] + chip[at] + other[0:128] * weights[t])
        rows.append(
            own[256:257, back] + core[256:257, at] + chip[256:257, at] + other[128:129, 0:128] * weights[t]
        )
    return blocks, rows


def sweep_kernel(flags, scaled, own, core, chip, other, near, message, to_half):
    blocks, rows = beside(flags[0], own, core, chip, other)
    new, new_rows = [], []
    for t in range(2):
        at = slice(t * 128, t * 128 + 128)
        near[at] = blocks[t]
        new.append(dot3(scaled[at], blocks[t]))
        message[at] = new[t]
        new_rows.append(dot(rows[t], scaled[at]))
    put_rows(near, *rows)
    put_rows(message, *new_rows)
    put_half(flags[0], to_half, new, new_rows)


def apply_kernel(flags, scaled, near, message, to_half):
    new, new_rows = [], []
    for t in range(2):
        at = slice(t * 128, t * 128 + 128)
        new.append(dot3(scaled[at], near[at]))
        message[at] = new[t]
        new_rows.append(dot(near[256:257, at], scaled[at]))
    put_rows(message, *new_rows)
    put_half(flags[0], to_half, new, new_rows)


def total_kernel(flags, near0, near1, near2, near3, own, core, chip, other, total):
    blocks, rows = beside(flags[0], own, core, chip, other)
    for t in range(2):
        at = slice(t * 128, t * 128 + 128)
        total[at] = ((near0[at] + near1[at]) + (near2[at] + near3[at])) + blocks[t]
        rows[t] = rows[t] + ((near0[256:257, at] + near1[256:257, at]) + (near2[256:257, at] + near3[256:257, at]))
    put_rows(total, *rows)


def leaf_kernel(inverse, rows, coupling, total, solved, pulled):
    for t in range(2):
        at = slice(t * 128, t * 128 + 128)
        weight = rows[2 + t : 3 + t]
        down = jnp.broadcast_to(weight, (128, 128)).T
        source = coupling[at].astype(F32) + jnp.concatenate([down] * 4, axis=1) * total[at]
        solved[at] = dot3(inverse[at], source)
        row = dot(rows[t : t + 1] + weight * total[256:257, at], inverse[at])
        pulled[0:8, at] = jnp.broadcast_to(row, (8, 128))


def ring_columns(ref, b, count):
    parts = [ref[0:256, ((b + m) % 4) * 128 : ((b + m) % 4) * 128 + 128] for m in range(count)]
    return jnp.concatenate(parts, axis=1)


def gram_home_kernel(inverse, rows, coupling, right, gram, gather, first):
    row = -jnp.concatenate([right[i : i + 1] for i in range(4)], axis=1)
    for t in range(2):
        at = slice(t * 128, t * 128 + 128)
        first[at] = dot3(inverse[at], coupling[at].astype(F32))
        row = row + dot(rows[t : t + 1], first[at])
    gather[0:8] = jnp.broadcast_to(row, (8, 512))
    high, low = split(first[...])
    for b in range(4):
        count = 3 if b < 2 else 2
        at = slice(b * 128, b * 128 + 128)
        left = coupling[0:256, at]
        part = None
        for piece in (high, low):
            wide = ring_columns(piece, b, count)
            term = lax.dot_general(left, wide, ((TN), ((), ())), preferred_element_type=F32)
            part = term if part is None else part + term
        gram[at, 0 : count * 128] = part
        if count == 2:
            gram[at, 256:384] = jnp.zeros((128, 128), F32)


def gram_early_kernel(known, known_gather, own, near, gram, gather):
    for b in range(4):
        count = 3 if b < 2 else 2
        at = slice(b * 128, b * 128 + 128)
        part = dot3(own[0:256, at], ring_columns(near, b, count), TN)
        gram[at, 0 : count * 128] = known[at, 0 : count * 128] + part
        if count == 2:
            gram[at, 256:384] = jnp.zeros((128, 128), F32)
    row = known_gather[0:1]
    for t in range(2):
        at = slice(t * 128, t * 128 + 128)
        row = row + dot(near[256:257, at], own[at])
    gather[0:8] = jnp.broadcast_to(row, (8, 512))


def gram_late_kernel(
    flags, gram, gather, own0, own2, near1, own2_core, chip, other, near2, keep, send, total, both, fields
):
    blocks, rows = beside(flags[0], own2, own2_core, chip, other)
    both[...] = own0[0:256] + own2[0:256]
    row = gather[0:1]
    for t in range(2):
        at = slice(t * 128, t * 128 + 128)
        near2[at] = blocks[t]
        fields[at] = near1[at] + blocks[t]
        row = row + dot(rows[t] + near1[256:257, at], both[at])
    put_rows(near2, *rows)
    for b in range(4):
        count = 3 if b < 2 else 2
        at = slice(b * 128, b * 128 + 128)
        part = gram[at, 0 : count * 128] + dot3(both[0:256, at], ring_columns(fields, b, count), TN)
        for m in range(4):
            for j in range(4):
                source = part[m * 32 + j * 8 : m * 32 + j * 8 + 8]
                total[j % 2, j // 2, b * 32 + m * 8 : b * 32 + m * 8 + 8, 0 : count * 128] = source
                if count == 2:
                    extra = jnp.zeros((8, 128), F32)
                    if b == 2 and m == 0 and j == 0:
                        four = jnp.concatenate([row[:, i * 128 : i * 128 + 128] for i in range(4)], axis=0)
                        extra = jnp.concatenate([four, jnp.zeros((4, 128), F32)], axis=0)
                    total[j % 2, j // 2, b * 32 + m * 8 : b * 32 + m * 8 + 8, 256:384] = extra
    keep[...] = total[flags[1]]
    send[...] = total[1 - flags[1]]


def parent_kernel(
    flags, mine, across_x, across_core, across_both, root_part, upper, solved, solved_row, held
):
    leaf = flags[2]
    held[:, leaf] = mine[...]
    held[:, leaf ^ 2] = across_x[...]
    held[:, leaf ^ 1] = across_core[...]
    held[:, leaf ^ 3] = across_both[...]

    def block(b, m):
        return held[4 * b : 4 * b + 4, :, :, m * 128 : m * 128 + 128].reshape(128, 128)

    entry = {}
    for b in range(4):
        for j in range(b, 4):
            entry[b, j] = block(3, 1).T if (b, j) == (0, 3) else block(b, j - b)
    rhs = [held[4 * b : 4 * b + 4, :, :, 384:640].reshape(128, 256) for b in range(4)]
    reduced = held[8, 0, :, 256:384]
    rows = [reduced[b : b + 1] for b in range(4)]
    part = jnp.zeros((256, 256), F32)
    part_row = jnp.zeros((1, 256), F32)
    upper[...] = jnp.zeros((384, 512), F32)
    for b in range(4):
        (inverse,) = inverses([entry[b, b]])
        wide = jnp.concatenate([entry[b, j] for j in range(b + 1, 4)] + [rhs[b]], axis=1)
        wide = dot(inverse, wide)
        span = (3 - b) * 128
        done = wide[:, span:]
        solved[b * 128 : b * 128 + 128] = done
        row = dot(rows[b], inverse)
        solved_row[0:8, b * 128 : b * 128 + 128] = jnp.broadcast_to(row, (8, 128))
        for i in range(b + 1, 4):
            left = entry[b, i]
            skip = (i - b - 1) * 128
            change = dot(left, wide[:, skip:], TN)
            for j in range(i, 4):
                entry[i, j] = entry[i, j] - change[:, (j - i) * 128 : (j - i) * 128 + 128]
            rhs[i] = rhs[i] - change[:, (4 - i) * 128 :]
            rows[i] = rows[i] - dot(row, left)
            upper[b * 128 : b * 128 + 128, i * 128 : i * 128 + 128] = wide[:, skip : skip + 128]
        part = part + dot3(rhs[b], done, TN)
        part_row = part_row + dot(row, rhs[b])
    root_part[0:128] = part[0:128, 0:128]
    root_part[128:256] = part[0:128, 128:256]
    root_part[256:384] = part[128:256, 128:256]
    root_part[384:388] = jnp.broadcast_to(part_row[:, 0:128], (4, 128))
    root_part[388:392] = jnp.broadcast_to(part_row[:, 128:256], (4, 128))


def back_kernel(upper, solved, solved_row, link_solved, vector):
    pieces, rows = [None] * 4, [None] * 4
    for b in range(3, -1, -1):
        at = slice(b * 128, b * 128 + 128)
        piece, row = solved[at], solved_row[0:1, at]
        if b < 3:
            after = upper[at, b * 128 + 128 : 512]
            piece = piece - dot(after, jnp.concatenate(pieces[b + 1 :], axis=0))
            row = row - dot(jnp.concatenate(rows[b + 1 :], axis=1), after, NT)
        pieces[b], rows[b] = piece, row
        link_solved[at] = piece
    vector[...] = jnp.broadcast_to(jnp.concatenate(rows, axis=1), (8, 512))


def reach_kernel(link_solved, vector, leaf_solved, pulled, reach, base):
    reach[...] = dot3(leaf_solved[...], link_solved[...])
    base[...] = jnp.broadcast_to(pulled[0:1] - dot(vector[0:1], leaf_solved[...], NT), (8, 256))


def root_kernel(
    flags, mine, opposite, below, above, matrix, right, link_solved, vector, reach, base, step, parent, move
):
    part = (mine[...] + opposite[...]) + (below[...] + above[...])
    side = matrix[0:128, 128:256] + part[128:256]
    (first,) = inverses([matrix[0:128, 0:128] + part[0:128]])
    pushed = dot(first, side)
    (second,) = inverses([matrix[128:256, 128:256] + part[256:384] - dot(side, pushed, TN)])
    head = dot(right[0:1, 0:128] - part[384:385], first)
    tail = dot(right[0:1, 128:256] - part[388:389] - dot(head, side), second)
    head = head - dot(tail, pushed, NT)
    root = jnp.concatenate([head, tail], axis=1)
    step[...] = root
    whole = vector[0:1] + dot(root, link_solved[...], NT)
    last = base[0:1] - dot(root, reach[...], NT)
    for t in range(2):
        move[t : t + 1] = last[:, t * 128 : t * 128 + 128]
    chosen = jnp.zeros((1, 128), F32)
    for b in range(4):
        chosen = chosen + jnp.where(flags[3] == b, whole[:, b * 128 : b * 128 + 128], 0.0)
    chosen = pltpu.roll(jnp.broadcast_to(chosen, (8, 128)), flags[4], 1)
    parent[...] = chosen[0:1, 0:32]


def neighbours(message, to_half):
    chip = lax.ppermute(message, AXES, TO_CHIP)
    other = lax.ppermute(to_half, AXES, TO_HALF)
    return lax.ppermute(message, AXES, TO_CORE), chip, other


def body(
    coupling, leaf_rhs, conductance, compressor, blocks, parent_of, parent_mat, parent_rhs, link, root_mat, root_rhs
):
    scen = lax.axis_index("scen")
    space = lax.axis_index("space")
    tm = lax.axis_index("tm")
    z = tm * 8 + space
    strip = space * 2 + tm
    quarter = ((z - Z_SHIFT) % 16) // 4
    core = scen % 2
    column = (scen // 2) % 2
    half = column ^ (quarter % 2)
    turn = (128 - (strip % 4) * 32) % 128
    flags = jnp.stack([half, core, scen % 4, strip // 4, turn]).astype(jnp.int32)

    weight = conductance[0] * (1.0 + compressor[0].astype(F32)[..., None]) * 0.5
    own_coupling = coupling[0].reshape(256, 512)
    rows = jnp.concatenate(
        [leaf_rhs[0].reshape(2, 128), weight.reshape(2, 128), jnp.zeros((4, 128), F32)], axis=0
    )
    field = lax.ppermute(own_coupling.astype(F32), AXES, MOVE_OUT)
    own_inverse, own_pack = call(invert_kernel, [(256, 128), (136, 128)], blocks[0].reshape(256, 128), rows)
    pack = lax.ppermute(own_pack, AXES, MOVE_OUT)

    label = parent_of[0]
    sibling = scen % 4
    row_block = strip // 4
    matrix_rows = lax.dynamic_slice(parent_mat, (label, sibling * 8, 0), (1, 8, 512))[0]
    matrix_rows = lax.dynamic_slice(
        jnp.concatenate([matrix_rows, matrix_rows], axis=1), (0, row_block * 128), (8, 384)
    )
    spare = (row_block >= 2) & (lax.broadcasted_iota(jnp.int32, (8, 384), 1) >= 256)
    matrix_rows = jnp.where(spare, 0.0, matrix_rows)
    link_rows = lax.dynamic_slice(link, (label, sibling * 8, 0), (1, 8, 256))[0]
    right = lax.dynamic_slice(parent_rhs, (label, 0), (1, 32))[0] * (sibling == 0).astype(F32)
    right = lax.dynamic_update_slice(jnp.zeros((512,), F32), right, (strip * 32,)).reshape(4, 128)
    right = jnp.concatenate([right, jnp.zeros((4, 128), F32)], axis=0)

    gram, gather = call(
        gram_home_kernel, [(512, 384), (8, 512)], own_inverse, rows, own_coupling, right,
        scratch=[pltpu.VMEM((256, 512), F32)],
    )
    pack, gram = lax.optimization_barrier((pack, gram))
    shapes = [(256, 128), (264, 512), (136, 512)]
    scaled, own0, half0 = call(start_kernel, shapes, flags, pack, field, scalars=1)
    shapes = [(264, 512), (264, 512), (136, 512)]
    near0, own1, half1 = call(sweep_kernel, shapes, flags, scaled, own0, *neighbours(own0, half0), scalars=1)
    around1 = neighbours(own1, half1)
    gram, gather = call(gram_early_kernel, [(512, 384), (8, 512)], gram, gather, own0, near0)
    near1, own2, half2 = call(sweep_kernel, shapes, flags, scaled, own1, *around1, scalars=1)
    near2, keep, send = call(
        gram_late_kernel,
        [(264, 512), (2, 128, 384), (2, 128, 384)],
        flags, gram, gather, own0, own2, near1, *neighbours(own2, half2),
        scalars=1,
        scratch=[pltpu.VMEM((2, 2, 128, 384), F32), pltpu.VMEM((256, 512), F32), pltpu.VMEM((256, 512), F32)],
    )
    own3, half3 = call(apply_kernel, shapes[1:], flags, scaled, near2, scalars=1)
    around3 = neighbours(own3, half3)
    theirs, _ = lax.optimization_barrier((lax.ppermute(send, "scen", flip(1)), own3))
    half_sum = (keep + theirs).reshape(32, 8, 384)
    shares = lax.all_to_all(half_sum, AXES, 0, 0, axis_index_groups=SAME_CORE)
    near3, own4, half4 = call(sweep_kernel, shapes, flags, scaled, own3, *around3, scalars=1)
    around4 = neighbours(own4, half4)
    shares, _ = lax.optimization_barrier((shares, own4))
    share = jnp.concatenate([jnp.sum(shares, axis=0) + matrix_rows, link_rows], axis=1)
    share = jnp.broadcast_to(share[None], (16, 8, 640))
    mine = lax.all_to_all(share, Z_AXES, 0, 0)
    (total,) = call(total_kernel, [(264, 512)], flags, near0, near1, near2, near3, own4, *around4, scalars=1)
    mine, total = lax.optimization_barrier((mine, total))
    across_x = lax.ppermute(mine, "scen", flip(2))
    across_core = lax.ppermute(mine, "scen", flip(1))
    across_both = lax.ppermute(across_x, "scen", flip(1))

    total = lax.ppermute(total, AXES, MOVE_BACK)
    leaf_solved, pulled = call(leaf_kernel, [(256, 512), (8, 256)], own_inverse, rows, own_coupling, total)

    part, upper, solved, solved_row = call(
        parent_kernel,
        [(392, 128), (384, 512), (512, 256), (8, 512)],
        flags, mine, across_x, across_core, across_both,
        scalars=1,
        scratch=[pltpu.VMEM((16, 4, 8, 640), F32)],
    )
    across = lax.ppermute(part, "scen", flip(4))
    link_solved, vector = call(back_kernel, [(512, 256), (8, 512)], upper, solved, solved_row)
    across, leaf_solved, link_solved = lax.optimization_barrier((across, leaf_solved, link_solved))
    part = part + across
    others = [lax.ppermute(part, "scen", [(i, (i + by) % 32) for i in range(32)]) for by in (16, 8, 24)]
    reach, base = call(reach_kernel, [(256, 256), (8, 256)], link_solved, vector, leaf_solved, pulled)
    others[2], reach = lax.optimization_barrier((others[2], reach))
    step, parent, move = call(
        root_kernel,
        [(1, 256), (1, 32), (2, 128)],
        flags, part, *others, root_mat, root_rhs.reshape(1, 256), link_solved, vector, reach, base,
        scalars=1,
    )
    return move.reshape(1, 2, 1, 128), parent, step.reshape(256)


def solution(mesh):
    return jax.shard_map(
        body,
        mesh=mesh,
        in_specs=(
            P("scen", "tm", "space", None, None),
            P("scen", "tm", "space", None),
            P("scen", "tm", "space", None),
            P("scen", "tm", "space"),
            P("scen", "tm", "space", None, None),
            P("scen"),
            P(None, ("space", "tm"), None),
            P(None, ("space", "tm")),
            P(None, ("space", "tm"), None),
            P(),
            P(),
        ),
        out_specs=(P("scen", "tm", "space", None), P("scen", ("space", "tm")), P()),
        check_vma=False,
    )
```
